128 devices in a mesh: brick: 16 (over x, y), slab: 8 (over z, core).
Axes of the slice: x: 4, y: 4, z: 4, core: 2. Of those that a mesh axis runs over, the one named last changes fastest.
Arguments:
- positions: float32 [16384, 3, 128], P(('brick', 'slab')), may hold values from 0 to 4
- charges: float32 [16384, 128], P(('brick', 'slab')), may hold values from 0.5 to 2
- drag: float32 [16384, 128], P(('brick', 'slab')), may hold values from 2 to 8
- right_side: float32 [16384, 128], P(('brick', 'slab')), may hold values from -2.5 to 6.5
- neighbours: int32 [16384, 4], P(('brick', 'slab')), may hold values from 0 to 16383, as said below
- owners: int32 [16384, 1], P(('brick', 'slab')), may hold values from 0 to 15; in each aligned block of 128 rows (0 to 127, 128 to 255, ...) at most 24 rows name the same one
Outputs:
- owned_solution: float32 [49152, 128], P(('brick', 'slab'))
- owned_residual: float32 [49152, 128], P(('brick', 'slab'))
The draws below stay inside these ranges and needn't reach their ends.
Inputs may be any that keep to these rules, and one draw needn't show every extreme that they name: A tile's neighbours lie on the same brick index and the same or an adjacent slab index; in each slot k pairing goes both ways (u is t's neighbour in slot k exactly when t is u's); never the tile itself. `owners`: among the 128 tiles of one device at most 24 name the same owner, a bound that some block reaches of them.
All inputs are finite; a program needn't handle non-finite values.
Results may differ from the reference program's by a relative error of at most 0.0009.
Values may be sent and summed in bfloat16 or wider, within the bound.
No kernel may reach another device: no remote copies, remote signals or barrier semaphores. Data moves between devices by JAX's collectives and lax.ppermute only.
A program may use at most 64 MiB of HBM per device.

```python
import math
import jax
import jax.numpy as jnp
import numpy as np
from jax import lax

TILE = 128
K = 4
TPD = 128
ITERS = 3
CAP = 24
SLOTS = 384
NT = 16384
N_BRICK = 16
N_SLAB = 8
DEVICES = 128


def draw_neighbours(key, part):
    tile_ids = jnp.arange(NT, dtype=jnp.int32)
    device = tile_ids // TPD
    within = tile_ids % TPD
    slab_of = device % N_SLAB
    columns = []
    for slot in range(K):
        subkeys = jax.random.split(jax.random.fold_in(key, 101 + slot), DEVICES)
        orders = jax.vmap(lambda subkey: jax.random.permutation(subkey, TPD))(subkeys).astype(jnp.int32)
        inverse = jnp.argsort(orders, axis=1).astype(jnp.int32)
        parity = slot % 2
        lower = (slab_of % 2 == parity) & (slab_of + 1 < N_SLAB)
        upper = ((slab_of + 1) % 2 == parity) & (slab_of >= 1)
        up_partner = (device + 1) * TPD + orders[device, within]
        down_partner = (device - 1) * TPD + inverse[device - 1, within]
        self_partner = device * TPD + orders[device, jnp.bitwise_xor(inverse[device, within], 1)]
        columns.append(jnp.where(lower, up_partner, jnp.where(upper, down_partner, self_partner)))
    return jnp.stack(columns, axis=1).astype(jnp.int32)


def draw_right_side(key, part):
    rough_key = jax.random.fold_in(key, 7)
    level_key = jax.random.fold_in(key, 11)
    rough = jnp.clip(jax.random.normal(rough_key, (NT, TILE), jnp.float32), -3.5, 3.5)
    level = jax.random.uniform(level_key, (NT, 1), jnp.float32, 1.0, 3.0)
    return (level + rough).astype(jnp.float32)


def steps_of(own_key, dims, pieces, least, largest):
    factor_of = 1.0
    for dim, parts in pieces:
        steps = jax.random.uniform(jax.random.fold_in(jax.random.fold_in(own_key, 6), dim), (parts,), jnp.float32, least / len(pieces), largest / len(pieces))
        factor_of = factor_of * jnp.repeat(jnp.exp(steps), dims[dim] // parts).reshape((-1,) + (1,) * (len(dims) - 1 - dim))
    return factor_of


def shared_out(own_key, own, number, rows, number_of, top, limit, slope):
    sequence = jax.random.permutation(own_key, number_of)
    crowded, common = shares(number_of, rows * top, limit, slope, True), shares(number_of, rows * top, limit, slope, False)
    places = jnp.arange(number_of)

    def named(tallies, rotation):
        used = int((tallies > 0).sum())
        fixed = max(1, used // 4)
        shifted = fixed + (places - fixed + rotation * (used - fixed)) % max(1, number_of - fixed)
        return jnp.zeros((number_of,), jnp.int32).at[sequence[jnp.where(places < fixed, places, shifted)]].set(jnp.asarray(tallies, jnp.int32))

    tallies = jnp.where(number % 4 == 0, named(crowded, number // 4), named(common, number - number // 4 - 1))
    mixed = jax.random.permutation(jax.random.fold_in(own, 3), number_of)
    donor, sink = mixed[0:number_of // 2 * 2:2], mixed[1:number_of // 2 * 2:2]
    slack = jnp.minimum(tallies[donor] - 1, limit - tallies[sink]) // 2
    slack = jnp.where((donor == sequence[0]) | (sink == sequence[0]) | (tallies[sink] == 0), 0, jnp.maximum(slack, 0))
    shifted = jax.random.randint(jax.random.fold_in(own, 4), (number_of // 2,), 0, 1 << 20) % (slack + 1)
    tallies = tallies.at[donor].add(-shifted).at[sink].add(shifted)
    items = jnp.searchsorted(jnp.cumsum(tallies), jnp.arange(rows * top), side="right").astype(jnp.int32)
    listing = items.reshape(top, rows).T
    listing = listing[jax.random.permutation(jax.random.fold_in(own, 1), rows)]
    rotation = jax.random.randint(jax.random.fold_in(own, 2), (rows, 1), 0, top)
    return jnp.take_along_axis(listing, (jnp.arange(top)[None, :] + rotation) % top, axis=1)


def shares(count, total, reach, slope, full):
    loads = [(1 << 20) // math.isqrt(grade ** slope) + 1 for grade in range(1, count + 1)]
    largest = reach if full else min(reach, max(-(-total // count), total * loads[0] // sum(loads)))
    least = 1 if total - largest >= count - 1 else 0
    counts, rest = [largest] + [least] * (count - 1), total - largest - least * (count - 1)
    while rest > 0:
        candidates = [i for i in range(1, count) if counts[i] < largest] or [i for i in range(1, count) if counts[i] < reach]
        whole, remaining = sum([loads[i] for i in candidates]), rest
        for i in candidates:
            extra = min(reach - counts[i], max(1, remaining * loads[i] // whole), rest)
            counts[i] = counts[i] + extra
            rest = rest - extra
    return np.array(counts)


def setup_inputs(seed: int = 0) -> dict:
    key_list = jax.random.split(jax.random.key(seed), 7)
    positions = jnp.clip(4.0 * jax.random.uniform(key_list[0], (NT, 3, TILE), jnp.float32) ** steps_of(key_list[0], (NT, 3, TILE), ((0, 128),), -0.2, 0.2), 0.0, 4.0)
    charges = jnp.clip(jnp.exp(math.log(2.0) - 1.3862944 * jax.random.uniform(key_list[1], (NT, TILE), jnp.float32) ** steps_of(key_list[1], (NT, TILE), ((0, 128),), -0.2, 0.2)), 0.5, 2.0)
    drag = jnp.clip(jnp.exp(math.log(8.0) - 1.3862944 * jax.random.uniform(key_list[2], (NT, TILE), jnp.float32) ** steps_of(key_list[2], (NT, TILE), ((0, 128),), -0.2, 0.2)), 2.0, 8.0)
    right_side = draw_right_side(jax.random.fold_in(key_list[6], 71), 0)
    neighbours = draw_neighbours(jax.random.fold_in(key_list[6], 71), 0)
    owners_keys = jax.random.split(jax.random.fold_in(key_list[5], 1), NT // TPD)
    owners_turns = jax.random.permutation(jax.random.fold_in(key_list[5], 3), NT // TPD)
    owners = jax.vmap(lambda own, number: shared_out(jax.random.fold_in(key_list[5], 2), own, number, TPD, N_BRICK, 1, CAP, 2))(owners_keys, owners_turns).reshape((NT, 1))
    return {"positions": positions, "charges": charges, "drag": drag, "right_side": right_side, "neighbours": neighbours, "owners": owners}


def couplings(own_tile, other_tiles, scale):
    delta_x = own_tile[:, None, 0, :, None] - other_tiles[:, :, 0, None, :]
    delta_y = own_tile[:, None, 1, :, None] - other_tiles[:, :, 1, None, :]
    delta_z = own_tile[:, None, 2, :, None] - other_tiles[:, :, 2, None, :]
    squared = delta_x * delta_x + delta_y * delta_y + delta_z * delta_z
    distance = jnp.sqrt(squared + 0.01)
    charge_product = own_tile[:, None, 3, :, None] * other_tiles[:, :, 3, None, :]
    return (1.0 / (squared + 0.5) + charge_product * jnp.exp(-distance)) * scale

def reference(positions, charges, drag, right_side, neighbours, owners):
    packed = jnp.concatenate([positions, charges[:, None, :]], axis=1)
    tile_ids = jnp.arange(NT, dtype=jnp.int32)
    index_all = jnp.concatenate([tile_ids[:, None], neighbours], axis=1)
    scale = 8.0 / ((K + 1) * TILE)
    first_slot = (jnp.arange(K + 1) == 0).astype(jnp.float32)
    self_mask = 1.0 - first_slot[:, None, None] * jnp.eye(TILE, dtype=jnp.float32)
    group_ids = jnp.arange(DEVICES, dtype=jnp.int32)

    def group_weights(group):
        rows = lax.dynamic_slice_in_dim(index_all, group * TPD, TPD, 0)
        own_tile = lax.dynamic_slice_in_dim(packed, group * TPD, TPD, 0)
        return couplings(own_tile, packed[rows], scale) * self_mask
    row_sums = lax.map(lambda group: lax.optimization_barrier(jnp.sum(group_weights(group), axis=(1, 3))), group_ids)
    diagonal = drag + row_sums.reshape(NT, TILE)

    def apply_matrix(direction):
        high_part = lax.optimization_barrier(direction.astype(jnp.bfloat16))
        low_part = lax.optimization_barrier((direction - high_part.astype(jnp.float32)).astype(jnp.bfloat16))

        def group_product(group):
            blocks = lax.optimization_barrier(group_weights(group).astype(jnp.bfloat16)).astype(jnp.float32)
            rows = lax.dynamic_slice_in_dim(index_all, group * TPD, TPD, 0)
            picked = high_part[rows].astype(jnp.float32) + low_part[rows].astype(jnp.float32)
            return jnp.einsum('tkac,tkc->ta', blocks, picked, precision=lax.Precision.HIGHEST)
        coupled = lax.map(group_product, group_ids).reshape(NT, TILE)
        return diagonal * direction - coupled
    solution = jnp.zeros_like(right_side)
    residual = right_side
    direction = right_side
    norm_now = jnp.sum(residual * residual)
    for iteration in range(ITERS):
        product = apply_matrix(direction)
        step_size = norm_now / jnp.sum(direction * product)
        solution = solution + step_size * direction
        residual = residual - step_size * product
        norm_next = jnp.sum(residual * residual)
        direction = residual + norm_next / norm_now * direction
        norm_now = norm_next
    owner_grid = owners[:, 0].reshape(DEVICES, TPD)
    matching = owner_grid[:, :, None] == owner_grid[:, None, :]
    earlier = jnp.arange(TPD)[None, :] < jnp.arange(TPD)[:, None]
    position = lax.optimization_barrier(jnp.sum((matching & earlier[None]).astype(jnp.int32), axis=2)).astype(jnp.int32)
    device = jnp.arange(DEVICES, dtype=jnp.int32)[:, None]
    home_brick = device // N_SLAB
    home_slab = device % N_SLAB
    target = ((owner_grid * N_SLAB + home_slab) * SLOTS + home_brick * CAP + position).reshape(NT).astype(jnp.int32)
    owned_solution = jnp.zeros((DEVICES * SLOTS, TILE), jnp.float32).at[target].set(solution)
    owned_residual = jnp.zeros((DEVICES * SLOTS, TILE), jnp.float32).at[target].set(residual)
    return (owned_solution, owned_residual)
```

```python
import functools

import jax
import jax.numpy as jnp
from jax import lax
from jax.experimental import pallas as pl
from jax.experimental.pallas import tpu as pltpu
from jax.sharding import PartitionSpec as P

ITERS = 3
SHIFT = 7.0
LOG2E = 1.4426950408889634
F32 = jnp.float32
BF16 = jnp.bfloat16
BOTH = ("brick", "slab")
PAIRS = {
    (0, 0): 0,
    (0, 1): 1,
    (1, 1): 2,
    (0, 2): 3,
    (1, 2): 4,
    (2, 2): 5,
    (0, 3): 6,
    (1, 3): 7,
    (2, 3): 8,
}
VMEM = pl.BlockSpec(memory_space=pltpu.VMEM)


def split3(value):
    high = value.astype(BF16)
    rest = value - high.astype(F32)
    middle = rest.astype(BF16)
    low = (rest - middle.astype(F32)).astype(BF16)
    return high, middle, low


def split2(value):
    high = value.astype(BF16).astype(F32)
    low = (value - high).astype(BF16).astype(F32)
    return high, low


def rows_at(ref, row, count):
    return ref[pl.ds(row, count, stride=8), :]


def put_rows(ref, row, value):
    ref[pl.ds(row, value.shape[0], stride=8), :] = value


def add_dots(row, vectors):
    lane = lax.broadcasted_iota(jnp.int32, (1, 128), 1)
    newest = len(vectors) - 1
    for (i, j), place in PAIRS.items():
        if j == newest or (newest == 1 and j == 0):
            product = vectors[i] * vectors[j]
            total = jnp.sum(jnp.sum(product, axis=0, keepdims=True), axis=1, keepdims=True)
            row = row + jnp.where(lane == place, total, 0.0)
    return row


def pack_kernel(pos_ref, charge_ref, force_ref, out_ref):
    count = charge_ref.shape[0]
    for j in range(3):
        out_ref[pl.ds(j * count, count), :] = pos_ref[:, j, :] - 2.0
    out_ref[pl.ds(3 * count, count), :] = jnp.log2(charge_ref[...])
    out_ref[pl.ds(4 * count, count), :] = force_ref[...]


def weights_kernel(
    scale, step_tiles, index_ref, own_ref, near_ref, far_ref, drag_ref,
    blocks_ref, vector_ref, diagonal_ref, row_ref, raw, mine, sums, images,
):
    step = pl.program_id(0)
    count = drag_ref.shape[0]
    square = LOG2E * LOG2E

    @pl.when(step == 0)
    def _():
        one = jnp.ones((count, 128), F32)
        zero = jnp.zeros((count, 128), F32)
        for part, ref in enumerate((own_ref, near_ref, far_ref)):
            base = part * count * 8
            x, y, z, charge, force = (ref[pl.ds(j * count, count), :] for j in range(5))
            norm = x * x + y * y + z * z
            high, low = split2(force)
            for j, value in enumerate((x, y, z, charge, norm, one, high, low)):
                put_rows(raw, base + j, value)
            if part == 0:
                first = (-2.0 / scale) * x, (-2.0 / scale) * y, (-2.0 / scale) * z
                rows = (*first, zero, one / scale, (norm + 0.5) / scale, zero, zero)
                second = (-2.0 * square) * x, (-2.0 * square) * y, (-2.0 * square) * z
                rows += (*second, zero, one * square, (norm + 0.01) * square, zero, zero)
                rows += (zero, zero, zero, one, zero, charge + jnp.log2(scale * one), zero, zero)
                for j, value in enumerate(rows):
                    mine[pl.ds(j, count, stride=24), :] = value

    same = lax.broadcasted_iota(jnp.int32, (128, 128), 0) == lax.broadcasted_iota(
        jnp.int32, (128, 128), 1
    )

    def tile(i, carry):
        t = step * step_tiles + i
        rights = []
        for j in range(3):
            high, middle, low = split3(mine[pl.ds(pl.multiple_of(t * 24 + 8 * j, 8), 8), :])
            rights.append(jnp.concatenate([high, middle, low, high, middle, high], axis=0))
        right = jnp.concatenate(rights, axis=1)
        total = jnp.zeros((8, 128), F32)
        image = jnp.zeros((8, 128), F32)
        for k in range(5):
            u = t if k == 0 else index_ref[t * 4 + k - 1]
            high, middle, low = split3(raw[pl.ds(pl.multiple_of(u * 8, 8), 8), :])
            left = jnp.concatenate([high, high, high, middle, middle, low], axis=0)
            terms = lax.dot_general(
                left, right, (((0,), (0,)), ((), ())), preferred_element_type=F32
            )
            inverse = pl.reciprocal(terms[:, :128], approx=False)
            shifted = terms[:, 128:256]
            distance = shifted * lax.rsqrt(shifted)
            weight = inverse + jnp.exp2(terms[:, 256:] - distance)
            if k == 0:
                weight = jnp.where(same, 0.0, weight)
            total = total + jnp.sum(weight.reshape(16, 8, 128), axis=0)
            block = weight.astype(BF16)
            blocks_ref[i, pl.ds(128 * k, 128), :] = block
            image = image + jnp.dot(high, block, preferred_element_type=F32)
        place = pl.ds(pl.multiple_of(t * 8, 8), 8)
        sums[place, :] = total
        images[place, :] = image
        return carry

    lax.fori_loop(0, step_tiles, tile, 0)

    @pl.when(step == pl.num_programs(0) - 1)
    def _():
        diagonal = drag_ref[...]
        for j in range(8):
            diagonal = diagonal + rows_at(sums, j, count)
        coupled = rows_at(images, 6, count) + rows_at(images, 7, count)
        force = own_ref[pl.ds(4 * count, count), :]
        vector = (diagonal - SHIFT) * force - coupled
        diagonal_ref[...] = diagonal
        vector_ref[...] = vector
        row_ref[...] = add_dots(jnp.zeros((1, 128), F32), [force, vector])


def weights(index, own, near, far, drag, scale, step_tiles):
    count = drag.shape[0]
    whole = lambda shape: pl.BlockSpec(shape, lambda i, *_: (0,) * len(shape))
    return pl.pallas_call(
        functools.partial(weights_kernel, scale, step_tiles),
        grid_spec=pltpu.PrefetchScalarGridSpec(
            num_scalar_prefetch=1,
            grid=(count // step_tiles,),
            in_specs=[whole(own.shape)] * 3 + [whole(drag.shape)],
            out_specs=[
                pl.BlockSpec((step_tiles, 640, 128), lambda i, *_: (i, 0, 0)),
                whole(drag.shape),
                whole(drag.shape),
                whole((1, 128)),
            ],
            scratch_shapes=[
                pltpu.VMEM((3 * count * 8, 128), F32),
                pltpu.VMEM((count * 24, 128), F32),
                pltpu.VMEM((count * 8, 128), F32),
                pltpu.VMEM((count * 8, 128), F32),
            ],
        ),
        out_shape=[
            jax.ShapeDtypeStruct((count, 640, 128), BF16),
            jax.ShapeDtypeStruct(drag.shape, F32),
            jax.ShapeDtypeStruct(drag.shape, F32),
            jax.ShapeDtypeStruct((1, 128), F32),
        ],
        name="weights",
    )(index, own, near, far, drag)


def image_kernel(
    step_tiles, history, slots, index_ref, blocks_ref, diagonal_ref, row_ref, near_ref, far_ref, *refs
):
    past = refs[:history]
    if slots:
        owner_column, owner_row = refs[history : history + 2]
        refs = refs[2:]
    if slots:
        out_ref, totals_ref, parts, images = refs[history:]
    else:
        vector_ref, totals_ref, parts, images = refs[history:]
    step = pl.program_id(0)
    count = diagonal_ref.shape[0]

    @pl.when(step == 0)
    def _():
        for part, ref in enumerate((past[-1], near_ref, far_ref)):
            high, low = split2(ref[...])
            put_rows(parts, part * count * 8, high)
            put_rows(parts, part * count * 8 + 1, low)

    def tile(i, carry):
        t = step * step_tiles + i
        lefts = []
        for k in range(5):
            u = t if k == 0 else index_ref[t * 4 + k - 1]
            lefts.append(parts[pl.ds(pl.multiple_of(u * 8, 8), 8), :].astype(BF16))
        left = jnp.concatenate(lefts, axis=1)
        images[pl.ds(pl.multiple_of(t * 8, 8), 8), :] = jnp.dot(
            left, blocks_ref[i], preferred_element_type=F32
        )
        return carry

    lax.fori_loop(0, step_tiles, tile, 0, unroll=2)

    @pl.when(step == pl.num_programs(0) - 1)
    def _():
        coupled = rows_at(images, 0, count) + rows_at(images, 1, count)
        vectors = [ref[...] for ref in past]
        vector = (diagonal_ref[...] - SHIFT) * vectors[-1] - coupled
        vectors.append(vector)
        row = add_dots(row_ref[...], vectors)
        if not slots:
            vector_ref[...] = vector
            totals_ref[...] = row
            return
        totals_ref[...] = jnp.broadcast_to(row, totals_ref.shape)
        owners, rows_each, _ = out_ref.shape
        each = rows_each // 4
        earlier = lax.broadcasted_iota(jnp.int32, (count, count), 0) < lax.broadcasted_iota(
            jnp.int32, (count, count), 1
        )
        matching = (owner_column[...] == owner_row[...]) & earlier
        position = jnp.sum(matching.astype(jnp.int32), axis=0, keepdims=True)
        target = owner_row[...] * each + position
        slot = lax.broadcasted_iota(jnp.int32, (owners * each, count), 0)
        chosen = (slot == target).astype(F32).astype(BF16)
        for j, value in enumerate(vectors):
            placed = sum(
                jnp.dot(chosen, piece, preferred_element_type=F32) for piece in split3(value)
            )
            for owner in range(owners):
                out_ref[owner, pl.ds(each * j, each), :] = placed[each * owner : each * (owner + 1)]


def image(index, blocks, diagonal, row, near, far, past, step_tiles, owners=None, slots=None):
    count = diagonal.shape[0]
    whole = lambda shape: pl.BlockSpec(shape, lambda i, *_: (0,) * len(shape))
    extra = [] if owners is None else list(owners)
    operands = [diagonal, row, near, far, *past, *extra]
    if owners is None:
        outs = [jax.ShapeDtypeStruct(diagonal.shape, F32), jax.ShapeDtypeStruct((1, 128), F32)]
    else:
        outs = [jax.ShapeDtypeStruct(slots[0], F32), jax.ShapeDtypeStruct(slots[1], F32)]
    return pl.pallas_call(
        functools.partial(image_kernel, step_tiles, len(past), owners is not None),
        grid_spec=pltpu.PrefetchScalarGridSpec(
            num_scalar_prefetch=1,
            grid=(count // step_tiles,),
            in_specs=[pl.BlockSpec((step_tiles, 640, 128), lambda i, *_: (i, 0, 0))]
            + [whole(value.shape) for value in operands],
            out_specs=[whole(value.shape) for value in outs],
            scratch_shapes=[
                pltpu.VMEM((3 * count * 8, 128), F32),
                pltpu.VMEM((count * 8, 128), F32),
            ],
        ),
        out_shape=outs,
        name="image",
    )(index, blocks, *operands)


def coefficients(totals):
    lane = lax.broadcasted_iota(jnp.int32, (1, 128), 1)
    gram = {}
    for (i, j), place in PAIRS.items():
        value = jnp.sum(jnp.where(lane == place, totals, 0.0), axis=1, keepdims=True)
        gram[i, j] = gram[j, i] = value

    def dot(a, b):
        return sum(x * sum(gram[i, j] * y for j, y in enumerate(b)) for i, x in enumerate(a))

    one = jnp.ones((1, 1), F32)
    zero = jnp.zeros((1, 1), F32)
    solution, residual, direction = [], [one], [one]
    norm = gram[0, 0]
    for iteration in range(ITERS):
        padded = direction + [zero]
        product = [SHIFT * value for value in padded]
        product = [value + (padded[j - 1] if j else zero) for j, value in enumerate(product)]
        step = norm / dot(direction, product)
        solution = [a + step * b for a, b in zip(solution + [zero], direction)]
        residual = [a - step * b for a, b in zip(residual + [zero], product)]
        if iteration < ITERS - 1:
            following = dot(residual, residual)
            direction = [a + (following / norm) * b for a, b in zip(residual, padded)]
            norm = following
    return solution, residual


def finish_kernel(arrived_ref, totals_ref, solution_ref, residual_ref):
    solution, residual = coefficients(jnp.sum(totals_ref[...], axis=0, keepdims=True))
    owners, rows_each, _ = arrived_ref.shape
    each = rows_each // 4
    for owner in range(owners):
        basis = [arrived_ref[owner, pl.ds(each * j, each), :] for j in range(4)]
        place = pl.ds(each * owner, each)
        solution_ref[place, :] = sum(a * v for a, v in zip(solution, basis))
        residual_ref[place, :] = sum(a * v for a, v in zip(residual, basis))


def local(positions, charges, drag, right_side, neighbours, owners):
    count = positions.shape[0]
    brick_count = lax.axis_size("brick")
    slab_count = lax.axis_size("slab")
    devices = brick_count * slab_count
    each = max(3, 3 * count // brick_count)
    slab_at = lax.axis_index("slab")
    first_tile = (lax.axis_index("brick") * slab_count + slab_at) * count
    inner = [(i, i ^ 1) for i in range(slab_count)]
    outer = [(i, i + 1) for i in range(1, slab_count - 1, 2)]
    outer = outer + [(target, source) for source, target in outer]

    packed = pl.pallas_call(
        pack_kernel,
        out_shape=jax.ShapeDtypeStruct((5 * count, 128), F32),
        in_specs=[VMEM] * 3,
        out_specs=VMEM,
        name="pack",
    )(positions, charges, right_side)

    offset = neighbours - first_tile
    layer = jnp.floor_divide(offset, count)
    partner = 1 - 2 * (slab_at % 2)
    part = jnp.where(layer == 0, 0, jnp.where(layer == partner, 1, 2))
    index = (offset - layer * count + part * count).reshape(-1)

    def both_sides(value):
        far = lax.ppermute(value, "slab", outer)
        near = lax.ppermute(value, "slab", inner)
        return near, far

    scale = 8.0 / ((neighbours.shape[1] + 1) * 128)
    near, far = both_sides(packed)
    blocks, first, diagonal, row = weights(index, packed, near, far, drag, scale, 16)
    near, far = both_sides(first)
    second, row = image(index, blocks, diagonal, row, near, far, [right_side, first], 16)
    near, far = both_sides(second)
    outgoing, totals = image(
        index,
        blocks,
        diagonal,
        row,
        near,
        far,
        [right_side, first, second],
        16,
        owners=(owners, owners.reshape(1, count)),
        slots=((brick_count, 4 * each, 128), (devices, 128)),
    )
    arrived = lax.all_to_all(outgoing, "brick", split_axis=0, concat_axis=0, tiled=True)
    totals = lax.all_to_all(
        totals.reshape(devices, 1, 128), BOTH, split_axis=0, concat_axis=0, tiled=True
    )
    shape = jax.ShapeDtypeStruct((brick_count * each, 128), F32)
    return pl.pallas_call(
        finish_kernel,
        out_shape=(shape, shape),
        in_specs=[VMEM] * 2,
        out_specs=(VMEM, VMEM),
        name="finish",
    )(arrived, totals.reshape(devices, 128))


def solution(mesh):
    placed = (
        P(BOTH, None, None),
        P(BOTH, None),
        P(BOTH, None),
        P(BOTH, None),
        P(BOTH, None),
        P(BOTH, None),
    )
    return jax.shard_map(
        local,
        mesh=mesh,
        in_specs=placed,
        out_specs=(P(BOTH, None), P(BOTH, None)),
        check_vma=False,
    )
```

```python
import functools

import jax
import jax.numpy as jnp
from jax import lax
from jax.experimental import pallas as pl
from jax.experimental.pallas import tpu as pltpu
from jax.sharding import PartitionSpec as P

ITERS = 3
SHIFT = 7.0
MIX = 6
UNROLL = 4
LOG2E = 1.4426950408889634
F32 = jnp.float32
BF16 = jnp.bfloat16
BOTH = ("brick", "slab")
PAIRS = {
    (0, 0): 0,
    (0, 1): 1,
    (1, 1): 2,
    (0, 2): 3,
    (1, 2): 4,
    (2, 2): 5,
    (0, 3): 6,
    (1, 3): 7,
    (2, 3): 8,
}
VMEM = pl.BlockSpec(memory_space=pltpu.VMEM)
SMEM = pl.BlockSpec(memory_space=pltpu.SMEM)
LIMIT = 12 << 20


def split3(value):
    high = value.astype(BF16)
    rest = value - high.astype(F32)
    middle = rest.astype(BF16)
    low = (rest - middle.astype(F32)).astype(BF16)
    return high, middle, low


def split2(value):
    high = value.astype(BF16).astype(F32)
    low = (value - high).astype(BF16).astype(F32)
    return high, low


def rows_at(ref, row, count):
    return ref[pl.ds(row, count, stride=8), :]


def put_rows(ref, row, value):
    ref[pl.ds(row, value.shape[0], stride=8), :] = value


def add_dots(row, vectors):
    lane = lax.broadcasted_iota(jnp.int32, (1, 128), 1)
    newest = len(vectors) - 1
    for (i, j), place in PAIRS.items():
        if j == newest or (newest == 1 and j == 0):
            product = vectors[i] * vectors[j]
            total = jnp.sum(jnp.sum(product, axis=0, keepdims=True), axis=1, keepdims=True)
            row = row + jnp.where(lane == place, total, 0.0)
    return row


def pack_kernel(pos_ref, charge_ref, force_ref, out_ref):
    count = charge_ref.shape[0]
    for j in range(3):
        out_ref[pl.ds(j * count, count), :] = pos_ref[:, j, :] - 2.0
    out_ref[pl.ds(3 * count, count), :] = jnp.log2(charge_ref[...])
    out_ref[pl.ds(4 * count, count), :] = force_ref[...]


def weights_kernel(
    scale, index_ref, own_ref, near_ref, far_ref, drag_ref,
    blocks_ref, vector_ref, diagonal_ref, row_ref, raw, mine, sums, images, even, odd,
):
    count = drag_ref.shape[0]
    square = LOG2E * LOG2E

    one = jnp.ones((count, 128), F32)
    zero = jnp.zeros((count, 128), F32)
    for part, ref in enumerate((own_ref, near_ref, far_ref)):
        base = part * count * 8
        x, y, z, charge, force = (ref[pl.ds(j * count, count), :] for j in range(5))
        norm = x * x + y * y + z * z
        high, low = split2(force)
        for j, value in enumerate((x, y, z, charge, norm, one, high, low)):
            put_rows(raw, base + j, value)
        if part == 0:
            doubled = (-2.0 * square) * x, (-2.0 * square) * y, (-2.0 * square) * z
            rows = (*doubled, zero, one * square, (norm + 0.5) * square, zero, zero)
            rows += (zero, zero, zero, one, zero, charge + jnp.log2(scale * one), zero, zero)
            for j, value in enumerate(rows):
                mine[pl.ds(j, count, stride=16), :] = value

    def other(t, k):
        return t if k == 0 else index_ref[t * 4 + k - 1]

    def terms(t):
        rights = []
        for j in range(2):
            high, middle, low = split3(mine[pl.ds(pl.multiple_of(t * 16 + 8 * j, 8), 8), :])
            rights.append(jnp.concatenate([high, middle, low, high, middle, high], axis=0))
        right = jnp.concatenate(rights, axis=1)
        lefts = []
        for k in range(5):
            u = other(t, k)
            high, middle, low = split3(raw[pl.ds(pl.multiple_of(u * 8, 8), 8), :])
            lefts.append(jnp.concatenate([high, high, high, middle, middle, low], axis=0))
        left = jnp.concatenate(lefts, axis=1)
        return lax.dot_general(
            left, right, (((0,), (0,)), ((), ())), preferred_element_type=F32
        )

    def block(t, source, incoming):
        totals = [None] * 4
        for pair in range(40):
            halves = []
            for half in range(2):
                chunk = 2 * pair + half
                place = pl.ds(8 * chunk, 8)
                wide = source[place, :128]
                shifted = wide - 0.49 * square
                if chunk % MIX == MIX - 1:
                    distance = shifted * lax.rsqrt(shifted)
                    inverse = pltpu.reciprocal(wide)
                else:
                    product = wide * shifted
                    root = lax.rsqrt(product * wide)
                    distance = product * root
                    inverse = root * distance
                weight = inverse * (square * scale) + jnp.exp2(source[place, 128:] - distance)
                if chunk < 16:
                    rows = lax.broadcasted_iota(jnp.int32, (8, 128), 0) + 8 * chunk
                    lanes = lax.broadcasted_iota(jnp.int32, (8, 128), 1)
                    weight = jnp.where(rows == lanes, 0.0, weight)
                past = totals[chunk % 4]
                totals[chunk % 4] = weight if past is None else past + weight
                halves.append(weight)
            blocks_ref[t, pl.ds(16 * pair, 16), :] = jnp.concatenate(halves, axis=0).astype(BF16)
            source[pl.ds(16 * pair, 16), :] = incoming[16 * pair : 16 * pair + 16]
        total = (totals[0] + totals[1]) + (totals[2] + totals[3])
        sums[pl.ds(pl.multiple_of(t * 8, 8), 8), :] = total

    def image(t):
        lefts = []
        for k in range(5):
            u = other(t, k)
            lefts.append(raw[pl.ds(pl.multiple_of(u * 8, 8), 8), :].astype(BF16))
        images[pl.ds(pl.multiple_of(t * 8, 8), 8), :] = jnp.dot(
            jnp.concatenate(lefts, axis=1), blocks_ref[t], preferred_element_type=F32
        )

    even[...] = terms(0)
    odd[...] = terms(1)

    def pair(j, carry):
        t = 2 * j
        image(jnp.maximum(t - 2, 0))
        image(jnp.maximum(t - 1, 0))
        block(t, even, terms(jnp.minimum(t + 2, count - 1)))
        block(t + 1, odd, terms(jnp.minimum(t + 3, count - 1)))
        return carry

    lax.fori_loop(0, count // 2, pair, 0)
    image(count - 2)
    image(count - 1)

    diagonal = drag_ref[...]
    for j in range(8):
        diagonal = diagonal + rows_at(sums, j, count)
    coupled = rows_at(images, 6, count) + rows_at(images, 7, count)
    force = own_ref[pl.ds(4 * count, count), :]
    vector = (diagonal - SHIFT) * force - coupled
    diagonal_ref[...] = diagonal
    vector_ref[...] = vector
    row_ref[...] = add_dots(jnp.zeros((1, 128), F32), [force, vector])


def weights(index, own, near, far, drag, scale):
    count = drag.shape[0]
    return pl.pallas_call(
        functools.partial(weights_kernel, scale),
        in_specs=[SMEM] + [VMEM] * 4,
        out_specs=[VMEM] * 4,
        out_shape=[
            pltpu.VMEM((count, 640, 128), BF16),
            jax.ShapeDtypeStruct(drag.shape, F32),
            jax.ShapeDtypeStruct(drag.shape, F32),
            jax.ShapeDtypeStruct((1, 128), F32),
        ],
        scratch_shapes=[
            pltpu.VMEM((3 * count * 8, 128), F32),
            pltpu.VMEM((count * 16, 128), F32),
            pltpu.VMEM((count * 8, 128), F32),
            pltpu.VMEM((count * 8, 128), F32),
            pltpu.VMEM((640, 256), F32),
            pltpu.VMEM((640, 256), F32),
        ],
        compiler_params=pltpu.CompilerParams(vmem_limit_bytes=LIMIT),
        name="weights",
    )(index, own, near, far, drag)


def image_kernel(history, slots, index_ref, blocks_ref, diagonal_ref, row_ref, near_ref, far_ref, *refs):
    past, refs = refs[:history], refs[history:]
    if slots:
        owner_column, owner_row, out_ref, totals_ref, parts, images = refs
    else:
        vector_ref, totals_ref, parts, images = refs
    count = diagonal_ref.shape[0]
    for part, ref in enumerate((past[-1], near_ref, far_ref)):
        high, low = split2(ref[...])
        put_rows(parts, part * count * 8, high)
        put_rows(parts, part * count * 8 + 1, low)

    def tile(t, carry):
        lefts = []
        for k in range(5):
            u = t if k == 0 else index_ref[t * 4 + k - 1]
            lefts.append(parts[pl.ds(pl.multiple_of(u * 8, 8), 8), :].astype(BF16))
        left = jnp.concatenate(lefts, axis=1)
        images[pl.ds(pl.multiple_of(t * 8, 8), 8), :] = jnp.dot(
            left, blocks_ref[t], preferred_element_type=F32
        )
        return carry

    lax.fori_loop(0, count, tile, 0, unroll=UNROLL)

    coupled = rows_at(images, 0, count) + rows_at(images, 1, count)
    vectors = [ref[...] for ref in past]
    vector = (diagonal_ref[...] - SHIFT) * vectors[-1] - coupled
    vectors.append(vector)
    row = add_dots(row_ref[...], vectors)
    if not slots:
        vector_ref[...] = vector
        totals_ref[...] = row
        return
    totals_ref[...] = jnp.broadcast_to(row, totals_ref.shape)
    owners, rows_each, _ = out_ref.shape
    each = rows_each // 4
    earlier = lax.broadcasted_iota(jnp.int32, (count, count), 0) < lax.broadcasted_iota(
        jnp.int32, (count, count), 1
    )
    matching = (owner_column[...] == owner_row[...]) & earlier
    position = jnp.sum(matching.astype(jnp.int32), axis=0, keepdims=True)
    target = owner_row[...] * each + position
    slot = lax.broadcasted_iota(jnp.int32, (owners * each, count), 0)
    chosen = (slot == target).astype(F32).astype(BF16)
    for j, value in enumerate(vectors):
        placed = sum(jnp.dot(chosen, piece, preferred_element_type=F32) for piece in split3(value))
        for owner in range(owners):
            out_ref[owner, pl.ds(each * j, each), :] = placed[each * owner : each * (owner + 1)]


def image(index, blocks, diagonal, row, near, far, past, owners=None, slots=None):
    count = diagonal.shape[0]
    extra = [] if owners is None else list(owners)
    operands = [blocks, diagonal, row, near, far, *past, *extra]
    if owners is None:
        outs = [jax.ShapeDtypeStruct(diagonal.shape, F32), jax.ShapeDtypeStruct((1, 128), F32)]
    else:
        outs = [jax.ShapeDtypeStruct(shape, F32) for shape in slots]
    return pl.pallas_call(
        functools.partial(image_kernel, len(past), owners is not None),
        in_specs=[SMEM] + [VMEM] * len(operands),
        out_specs=[VMEM] * len(outs),
        out_shape=outs,
        scratch_shapes=[
            pltpu.VMEM((3 * count * 8, 128), F32),
            pltpu.VMEM((count * 8, 128), F32),
        ],
        compiler_params=pltpu.CompilerParams(vmem_limit_bytes=LIMIT),
        name="image",
    )(index, *operands)


def coefficients(totals):
    lane = lax.broadcasted_iota(jnp.int32, (1, 128), 1)
    gram = {}
    for (i, j), place in PAIRS.items():
        value = jnp.sum(jnp.where(lane == place, totals, 0.0), axis=1, keepdims=True)
        gram[i, j] = gram[j, i] = value

    def dot(a, b):
        return sum(x * sum(gram[i, j] * y for j, y in enumerate(b)) for i, x in enumerate(a))

    one = jnp.ones((1, 1), F32)
    zero = jnp.zeros((1, 1), F32)
    solution, residual, direction = [], [one], [one]
    norm = gram[0, 0]
    for iteration in range(ITERS):
        padded = direction + [zero]
        product = [SHIFT * value for value in padded]
        product = [value + (padded[j - 1] if j else zero) for j, value in enumerate(product)]
        step = norm / dot(direction, product)
        solution = [a + step * b for a, b in zip(solution + [zero], direction)]
        residual = [a - step * b for a, b in zip(residual + [zero], product)]
        if iteration < ITERS - 1:
            following = dot(residual, residual)
            direction = [a + (following / norm) * b for a, b in zip(residual, padded)]
            norm = following
    return solution, residual


def finish_kernel(arrived_ref, totals_ref, solution_ref, residual_ref):
    solution, residual = coefficients(jnp.sum(totals_ref[...], axis=0, keepdims=True))
    owners, rows_each, _ = arrived_ref.shape
    each = rows_each // 4
    for owner in range(owners):
        basis = [arrived_ref[owner, pl.ds(each * j, each), :] for j in range(4)]
        place = pl.ds(each * owner, each)
        solution_ref[place, :] = sum(a * v for a, v in zip(solution, basis))
        residual_ref[place, :] = sum(a * v for a, v in zip(residual, basis))


def local(positions, charges, drag, right_side, neighbours, owners):
    count = positions.shape[0]
    brick_count = lax.axis_size("brick")
    slab_count = lax.axis_size("slab")
    devices = brick_count * slab_count
    each = max(3, 3 * count // brick_count)
    slab_at = lax.axis_index("slab")
    first_tile = (lax.axis_index("brick") * slab_count + slab_at) * count
    inner = [(i, i ^ 1) for i in range(slab_count)]
    outer = [(i, i + 1) for i in range(1, slab_count - 1, 2)]
    outer = outer + [(target, source) for source, target in outer]

    packed = pl.pallas_call(
        pack_kernel,
        out_shape=jax.ShapeDtypeStruct((5 * count, 128), F32),
        in_specs=[VMEM] * 3,
        out_specs=VMEM,
        compiler_params=pltpu.CompilerParams(vmem_limit_bytes=LIMIT),
        name="pack",
    )(positions, charges, right_side)

    offset = neighbours - first_tile
    layer = jnp.floor_divide(offset, count)
    partner = 1 - 2 * (slab_at % 2)
    part = jnp.where(layer == 0, 0, jnp.where(layer == partner, 1, 2))
    index = (offset - layer * count + part * count).reshape(-1)

    def both_sides(value):
        far = lax.ppermute(value, "slab", outer)
        near = lax.ppermute(value, "slab", inner)
        return near, far

    scale = 8.0 / ((neighbours.shape[1] + 1) * 128)
    near, far = both_sides(packed)
    blocks, first, diagonal, row = weights(index, packed, near, far, drag, scale)
    near, far = both_sides(first)
    second, row = image(index, blocks, diagonal, row, near, far, [right_side, first])
    near, far = both_sides(second)
    outgoing, totals = image(
        index,
        blocks,
        diagonal,
        row,
        near,
        far,
        [right_side, first, second],
        owners=(owners, owners.reshape(1, count)),
        slots=((brick_count, 4 * each, 128), (devices, 128)),
    )
    arrived = lax.all_to_all(outgoing, "brick", split_axis=0, concat_axis=0, tiled=True)
    totals = lax.all_to_all(
        totals.reshape(devices, 1, 128), BOTH, split_axis=0, concat_axis=0, tiled=True
    )
    shape = jax.ShapeDtypeStruct((brick_count * each, 128), F32)
    return pl.pallas_call(
        finish_kernel,
        out_shape=(shape, shape),
        in_specs=[VMEM] * 2,
        out_specs=(VMEM, VMEM),
        compiler_params=pltpu.CompilerParams(vmem_limit_bytes=LIMIT),
        name="finish",
    )(arrived, totals.reshape(devices, 128))


def solution(mesh):
    placed = (
        P(BOTH, None, None),
        P(BOTH, None),
        P(BOTH, None),
        P(BOTH, None),
        P(BOTH, None),
        P(BOTH, None),
    )
    return jax.shard_map(
        local,
        mesh=mesh,
        in_specs=placed,
        out_specs=(P(BOTH, None), P(BOTH, None)),
        check_vma=False,
    )
```

```python
import functools

import jax
import jax.numpy as jnp
from jax import lax
from jax.experimental import pallas as pl
from jax.experimental.pallas import tpu as pltpu
from jax.sharding import PartitionSpec as P

ITERS = 3
SHIFT = 7.0
MIX = 6
UNROLL = 4
LOG2E = 1.4426950408889634
F32 = jnp.float32
BF16 = jnp.bfloat16
BOTH = ("brick", "slab")
PAIRS = {
    (0, 0): 0,
    (0, 1): 1,
    (1, 1): 2,
    (0, 2): 3,
    (1, 2): 4,
    (2, 2): 5,
    (0, 3): 6,
    (1, 3): 7,
    (2, 3): 8,
}
VMEM = pl.BlockSpec(memory_space=pltpu.VMEM)
SMEM = pl.BlockSpec(memory_space=pltpu.SMEM)
HBM = pl.BlockSpec(memory_space=pltpu.HBM)
LIMIT = 12 << 20


def in_hbm(value):
    return pltpu.with_memory_space_constraint(value, pltpu.HBM)


def split3(value):
    high = value.astype(BF16)
    rest = value - high.astype(F32)
    middle = rest.astype(BF16)
    low = (rest - middle.astype(F32)).astype(BF16)
    return high, middle, low


def split2(value):
    high = value.astype(BF16).astype(F32)
    low = (value - high).astype(BF16).astype(F32)
    return high, low


def rows_at(ref, row, count):
    return ref[pl.ds(row, count, stride=8), :]


def put_rows(ref, row, value):
    ref[pl.ds(row, value.shape[0], stride=8), :] = value


def add_dots(row, vectors):
    lane = lax.broadcasted_iota(jnp.int32, (1, 128), 1)
    newest = len(vectors) - 1
    for (i, j), place in PAIRS.items():
        if j == newest or (newest == 1 and j == 0):
            product = vectors[i] * vectors[j]
            total = jnp.sum(jnp.sum(product, axis=0, keepdims=True), axis=1, keepdims=True)
            row = row + jnp.where(lane == place, total, 0.0)
    return row


def pack_kernel(each, pos_hbm, charge_hbm, force_hbm, owner_hbm, out_ref, target_ref, charge, owner, sems):
    count = charge.shape[0]
    copies = [
        pltpu.make_async_copy(source, target, sems.at[j])
        for j, (source, target) in enumerate(
            (
                (pos_hbm, out_ref.at[pl.ds(0, 3)]),
                (charge_hbm, charge),
                (force_hbm, out_ref.at[4]),
                (owner_hbm, owner),
            )
        )
    ]
    for copy in copies:
        copy.start()
    for copy in copies:
        copy.wait()
    out_ref[pl.ds(0, 3)] = out_ref[pl.ds(0, 3)] - 2.0
    out_ref[3] = jnp.log2(charge[...])
    owners = jnp.broadcast_to(owner[...].astype(F32), (count, count))
    earlier = lax.broadcasted_iota(jnp.int32, (count, count), 0) < lax.broadcasted_iota(
        jnp.int32, (count, count), 1
    )
    matching = jnp.where((owners.T == owners) & earlier, 1.0, 0.0)
    position = jnp.sum(matching, axis=0, keepdims=True).astype(jnp.int32)
    target_ref[...] = owner[...] * each + position


def weights_kernel(scale, first, blocks_count, index_ref, planes, blocks_ref, scratch, finish):
    raw, mine, sums, images, even, odd = scratch
    count = mine.shape[0] // 16
    square = LOG2E * LOG2E
    width = 128 * blocks_count
    one = jnp.ones((count, 128), F32)
    zero = jnp.zeros((count, 128), F32)
    for part, ref in enumerate(planes):
        base = part * count * 8
        x, y, z, charge, force = (ref[j] for j in range(5))
        norm = x * x + y * y + z * z
        high, low = split2(force)
        for j, value in enumerate((x, y, z, charge, norm, one, high, low)):
            put_rows(raw, base + j, value)
        if part == 0:
            doubled = (-2.0 * square) * x, (-2.0 * square) * y, (-2.0 * square) * z
            rows = (*doubled, zero, one * square, (norm + 0.5) * square, zero, zero)
            rows += (zero, zero, zero, one, zero, charge + jnp.log2(scale * one), zero, zero)
            for j, value in enumerate(rows):
                mine[pl.ds(j, count, stride=16), :] = value

    def entries(t):
        for k in range(blocks_count):
            u = t if first + k == 0 else index_ref[t * 4 + first + k - 1]
            yield raw[pl.ds(pl.multiple_of(u * 8, 8), 8), :]

    def terms(t):
        rights = []
        for j in range(2):
            high, middle, low = split3(mine[pl.ds(pl.multiple_of(t * 16 + 8 * j, 8), 8), :])
            rights.append(jnp.concatenate([high, middle, low, high, middle, high], axis=0))
        right = jnp.concatenate(rights, axis=1)
        lefts = []
        for value in entries(t):
            high, middle, low = split3(value)
            lefts.append(jnp.concatenate([high, high, high, middle, middle, low], axis=0))
        left = jnp.concatenate(lefts, axis=1)
        return lax.dot_general(
            left, right, (((0,), (0,)), ((), ())), preferred_element_type=F32
        )

    def block(t, source, incoming):
        totals = [None] * 4
        for pair in range(width // 16):
            halves = []
            for half in range(2):
                chunk = 2 * pair + half
                place = pl.ds(8 * chunk, 8)
                wide = source[place, :128]
                shifted = wide - 0.49 * square
                if chunk % MIX == MIX - 1:
                    distance = shifted * lax.rsqrt(shifted)
                    inverse = pltpu.reciprocal(wide)
                else:
                    product = wide * shifted
                    root = lax.rsqrt(product * wide)
                    distance = product * root
                    inverse = root * distance
                weight = inverse * (square * scale) + jnp.exp2(source[place, 128:] - distance)
                if first == 0 and chunk < 16:
                    rows = lax.broadcasted_iota(jnp.int32, (8, 128), 0) + 8 * chunk
                    lanes = lax.broadcasted_iota(jnp.int32, (8, 128), 1)
                    weight = jnp.where(rows == lanes, 0.0, weight)
                past = totals[chunk % 4]
                totals[chunk % 4] = weight if past is None else past + weight
                halves.append(weight)
            blocks_ref[t, pl.ds(16 * pair, 16), :] = jnp.concatenate(halves, axis=0).astype(BF16)
            source[pl.ds(16 * pair, 16), :] = incoming[16 * pair : 16 * pair + 16]
        total = (totals[0] + totals[1]) + (totals[2] + totals[3])
        sums[pl.ds(pl.multiple_of(t * 8, 8), 8), :] = total

    def image(t):
        left = jnp.concatenate([value.astype(BF16) for value in entries(t)], axis=1)
        images[pl.ds(pl.multiple_of(t * 8, 8), 8), :] = jnp.dot(
            left, blocks_ref[t], preferred_element_type=F32
        )

    even[...] = terms(0)
    odd[...] = terms(1)

    def pair(j, carry):
        t = 2 * j
        image(jnp.maximum(t - 2, 0))
        image(jnp.maximum(t - 1, 0))
        block(t, even, terms(jnp.minimum(t + 2, count - 1)))
        block(t + 1, odd, terms(jnp.minimum(t + 3, count - 1)))
        return carry

    lax.fori_loop(0, count // 2, pair, 0)
    image(count - 2)
    image(count - 1)
    total = rows_at(sums, 0, count)
    for j in range(1, 8):
        total = total + rows_at(sums, j, count)
    finish(total, rows_at(images, 6, count) + rows_at(images, 7, count))


def weights_scratch(count, parts, blocks_count):
    return [
        pltpu.VMEM((parts * count * 8, 128), F32),
        pltpu.VMEM((count * 16, 128), F32),
        pltpu.VMEM((count * 8, 128), F32),
        pltpu.VMEM((count * 8, 128), F32),
        pltpu.VMEM((128 * blocks_count, 256), F32),
        pltpu.VMEM((128 * blocks_count, 256), F32),
    ]


def own_kernel(scale, own_ref, blocks_ref, total_ref, image_ref, *scratch):
    def finish(total, coupled):
        total_ref[...] = total
        image_ref[...] = coupled

    weights_kernel(scale, 0, 1, None, [own_ref], blocks_ref, scratch, finish)


def own_weights(own, scale):
    count = own.shape[1]
    plane = jax.ShapeDtypeStruct((count, 128), F32)
    return pl.pallas_call(
        functools.partial(own_kernel, scale),
        in_specs=[VMEM],
        out_specs=[VMEM] * 3,
        out_shape=[pltpu.VMEM((count, 128, 128), BF16), plane, plane],
        scratch_shapes=weights_scratch(count, 1, 1),
        compiler_params=pltpu.CompilerParams(vmem_limit_bytes=LIMIT),
        cost_estimate=pl.CostEstimate(
            flops=count * 128 * 128 * 600, bytes_accessed=1 << 20, transcendentals=count * 128 * 256
        ),
        name="own_weights",
    )(own)


def other_kernel(
    scale, blocks_count, index_ref, own_ref, near_ref, far_ref, total_ref, image_ref, drag_hbm,
    blocks_ref, vector_ref, diagonal_ref, row_ref, drag, sem, *scratch,
):
    copy = pltpu.make_async_copy(drag_hbm, drag, sem)
    copy.start()

    def finish(total, coupled):
        copy.wait()
        diagonal = drag[...] + total_ref[...] + total
        force = own_ref[4]
        vector = (diagonal - SHIFT) * force - (image_ref[...] + coupled)
        diagonal_ref[...] = diagonal
        vector_ref[...] = vector
        row_ref[...] = add_dots(jnp.zeros((1, 128), F32), [force, vector])

    planes = [own_ref, near_ref, far_ref]
    weights_kernel(scale, 1, blocks_count, index_ref, planes, blocks_ref, scratch, finish)


def other_weights(index, own, near, far, total, image, drag, scale, blocks_count):
    count = drag.shape[0]
    plane = jax.ShapeDtypeStruct((count, 128), F32)
    return pl.pallas_call(
        functools.partial(other_kernel, scale, blocks_count),
        in_specs=[SMEM] + [VMEM] * 5 + [HBM],
        out_specs=[VMEM] * 4,
        out_shape=[
            pltpu.VMEM((count, 128 * blocks_count, 128), BF16),
            plane,
            plane,
            jax.ShapeDtypeStruct((1, 128), F32),
        ],
        scratch_shapes=[
            pltpu.VMEM((count, 128), F32),
            pltpu.SemaphoreType.DMA,
            *weights_scratch(count, 3, blocks_count),
        ],
        compiler_params=pltpu.CompilerParams(vmem_limit_bytes=LIMIT),
        name="other_weights",
    )(index, own, near, far, total, image, in_hbm(drag))


def image_kernel(
    history, index_ref, own_blocks, blocks_ref, diagonal_ref, row_ref, near_ref, far_ref, own_ref, *refs
):
    past, refs = [own_ref.at[4], *refs[:history]], refs[history:]
    vector_ref, totals_ref, parts, images = refs
    count = diagonal_ref.shape[0]
    for part, ref in enumerate((past[-1], near_ref, far_ref)):
        high, low = split2(ref[...])
        put_rows(parts, part * count * 8, high)
        put_rows(parts, part * count * 8 + 1, low)

    def tile(t, carry):
        lefts = []
        for k in range(1 + blocks_ref.shape[1] // 128):
            u = t if k == 0 else index_ref[t * 4 + k - 1]
            lefts.append(parts[pl.ds(pl.multiple_of(u * 8, 8), 8), :].astype(BF16))
        left = jnp.concatenate(lefts[1:], axis=1)
        value = jnp.dot(left, blocks_ref[t], preferred_element_type=F32)
        value = value + jnp.dot(lefts[0], own_blocks[t], preferred_element_type=F32)
        images[pl.ds(pl.multiple_of(t * 8, 8), 8), :] = value
        return carry

    lax.fori_loop(0, count, tile, 0, unroll=UNROLL)
    coupled = rows_at(images, 0, count) + rows_at(images, 1, count)
    vectors = [ref[...] for ref in past]
    vector = (diagonal_ref[...] - SHIFT) * vectors[-1] - coupled
    vectors.append(vector)
    vector_ref[...] = vector
    totals_ref[...] = add_dots(row_ref[...], vectors)


def image(index, blocks, diagonal, row, near, far, own, past):
    count = diagonal.shape[0]
    operands = [*blocks, diagonal, row, near, far, own, *past]
    return pl.pallas_call(
        functools.partial(image_kernel, len(past)),
        in_specs=[SMEM] + [VMEM] * len(operands),
        out_specs=[VMEM] * 2,
        out_shape=[
            jax.ShapeDtypeStruct(diagonal.shape, F32),
            jax.ShapeDtypeStruct(row.shape, F32),
        ],
        scratch_shapes=[
            pltpu.VMEM((3 * count * 8, 128), F32),
            pltpu.VMEM((count * 8, 128), F32),
        ],
        compiler_params=pltpu.CompilerParams(vmem_limit_bytes=LIMIT),
        name="image",
    )(index, *operands)


def slots_kernel(target_ref, own_ref, first_ref, second_ref, third_ref, out_ref):
    owners, rows_each, _ = out_ref.shape
    count = first_ref.shape[0]
    each = (rows_each - 8) // 4
    slot = lax.broadcasted_iota(jnp.int32, (owners * each, count), 0)
    chosen = (slot == target_ref[...]).astype(F32).astype(BF16)
    for j, ref in enumerate((own_ref.at[4], first_ref, second_ref, third_ref)):
        value = ref[...]
        placed = sum(jnp.dot(chosen, piece, preferred_element_type=F32) for piece in split3(value))
        for owner in range(owners):
            out_ref[owner, pl.ds(each * j, each), :] = placed[each * owner : each * (owner + 1)]


def join_kernel(parts_ref, *refs):
    sums, (_, out_ref) = refs[:-2], refs[-2:]
    row = parts_ref[...]
    for ref in sums:
        row = row + ref[...]
    owners, rows_each, _ = out_ref.shape
    for owner in range(owners):
        out_ref[owner, pl.ds(rows_each - 8, 8), :] = jnp.broadcast_to(row, (8, 128))


def coefficients(totals):
    lane = lax.broadcasted_iota(jnp.int32, (1, 128), 1)
    gram = {}
    for (i, j), place in PAIRS.items():
        value = jnp.sum(jnp.where(lane == place, totals, 0.0), axis=1, keepdims=True)
        gram[i, j] = gram[j, i] = value

    def dot(a, b):
        return sum(x * sum(gram[i, j] * y for j, y in enumerate(b)) for i, x in enumerate(a))

    one = jnp.ones((1, 1), F32)
    zero = jnp.zeros((1, 1), F32)
    solution, residual, direction = [], [one], [one]
    norm = gram[0, 0]
    for iteration in range(ITERS):
        padded = direction + [zero]
        product = [SHIFT * value for value in padded]
        product = [value + (padded[j - 1] if j else zero) for j, value in enumerate(product)]
        step = norm / dot(direction, product)
        solution = [a + step * b for a, b in zip(solution + [zero], direction)]
        residual = [a - step * b for a, b in zip(residual + [zero], product)]
        if iteration < ITERS - 1:
            following = dot(residual, residual)
            direction = [a + (following / norm) * b for a, b in zip(residual, padded)]
            norm = following
    return solution, residual


def finish_kernel(arrived_ref, solution_ref, residual_ref):
    owners, rows_each, _ = arrived_ref.shape
    each = (rows_each - 8) // 4
    totals = sum(arrived_ref[owner, pl.ds(rows_each - 8, 8), :] for owner in range(owners))
    solution, residual = coefficients(totals[:1])
    for owner in range(owners):
        basis = [arrived_ref[owner, pl.ds(each * j, each), :] for j in range(4)]
        place = pl.ds(each * owner, each)
        solution_ref[place, :] = sum(a * v for a, v in zip(solution, basis))
        residual_ref[place, :] = sum(a * v for a, v in zip(residual, basis))


def local(positions, charges, drag, right_side, neighbours, owners):
    count = positions.shape[0]
    brick_count = lax.axis_size("brick")
    slab_count = lax.axis_size("slab")
    each = max(3, 3 * count // brick_count)
    slab_at = lax.axis_index("slab")
    first_tile = (lax.axis_index("brick") * slab_count + slab_at) * count
    inner = [(i, i ^ 1) for i in range(slab_count)]
    outer = [(i, i + 1) for i in range(1, slab_count - 1, 2)]
    outer = outer + [(target, source) for source, target in outer]

    packed, target = pl.pallas_call(
        functools.partial(pack_kernel, each),
        out_shape=[
            jax.ShapeDtypeStruct((5, count, 128), F32),
            jax.ShapeDtypeStruct((1, count), jnp.int32),
        ],
        in_specs=[HBM] * 4,
        out_specs=[VMEM] * 2,
        scratch_shapes=[
            pltpu.VMEM((count, 128), F32),
            pltpu.VMEM((1, count), jnp.int32),
            pltpu.SemaphoreType.DMA((4,)),
        ],
        compiler_params=pltpu.CompilerParams(vmem_limit_bytes=LIMIT),
        name="pack",
    )(*map(in_hbm, (jnp.transpose(positions, (1, 0, 2)), charges, right_side, owners.reshape(1, count))))

    offset = neighbours - first_tile
    layer = jnp.floor_divide(offset, count)
    partner = 1 - 2 * (slab_at % 2)
    part = jnp.where(layer == 0, 0, jnp.where(layer == partner, 1, 2))
    index = (offset - layer * count + part * count).reshape(-1)

    def both_sides(value):
        far = lax.ppermute(value, "slab", outer)
        near = lax.ppermute(value, "slab", inner)
        return near, far

    scale = 8.0 / ((neighbours.shape[1] + 1) * 128)
    entries = neighbours.shape[1]
    near, far = both_sides(packed)
    own_blocks, total, coupled = own_weights(packed, scale)
    blocks, first, diagonal, row = other_weights(
        index, packed, near, far, total, coupled, drag, scale, entries
    )
    blocks = own_blocks, blocks
    near, far = both_sides(first)
    second, row = image(index, blocks, diagonal, row, near, far, packed, [first])
    near, far = both_sides(second)
    third, row = image(index, blocks, diagonal, row, near, far, packed, [first, second])
    row = row + lax.ppermute(row, "slab", inner)
    around = [
        lax.ppermute(row, "slab", [(i, (i + step) % slab_count) for i in range(slab_count)])
        for step in (slab_count // 2, *(x for x in range(2, slab_count, 2) if x != slab_count // 2))
    ]
    outgoing = jax.ShapeDtypeStruct((brick_count, 4 * each + 8, 128), F32)
    params = pltpu.CompilerParams(vmem_limit_bytes=LIMIT)
    basis = pl.pallas_call(
        slots_kernel,
        out_shape=outgoing,
        in_specs=[VMEM] * 5,
        out_specs=VMEM,
        compiler_params=params,
        cost_estimate=pl.CostEstimate(flops=1 << 30, bytes_accessed=1 << 20, transcendentals=0),
        name="slots",
    )(target, packed, first, second, third)
    outgoing = pl.pallas_call(
        join_kernel,
        out_shape=outgoing,
        in_specs=[VMEM] * (2 + len(around)),
        out_specs=VMEM,
        input_output_aliases={1 + len(around): 0},
        compiler_params=params,
        name="join",
    )(row, *around, basis)
    arrived = lax.all_to_all(outgoing, "brick", split_axis=0, concat_axis=0, tiled=True)
    shape = jax.ShapeDtypeStruct((brick_count * each, 128), F32)
    return pl.pallas_call(
        finish_kernel,
        out_shape=(shape, shape),
        in_specs=[VMEM],
        out_specs=(VMEM, VMEM),
        compiler_params=pltpu.CompilerParams(vmem_limit_bytes=LIMIT),
        name="finish",
    )(arrived)


def solution(mesh):
    placed = (
        P(BOTH, None, None),
        P(BOTH, None),
        P(BOTH, None),
        P(BOTH, None),
        P(BOTH, None),
        P(BOTH, None),
    )
    step = jax.shard_map(
        local,
        mesh=mesh,
        in_specs=placed,
        out_specs=(P(BOTH, None), P(BOTH, None)),
        check_vma=False,
    )
    return step
```

```python
import functools

import jax
import jax.numpy as jnp
from jax import lax
from jax.experimental import pallas as pl
from jax.experimental.pallas import tpu as pltpu
from jax.sharding import PartitionSpec as P

ITERS = 3
SHIFT = 7.0
MIX = 7
UNROLL = 64
GROUP = 8
OWN_GROUP = 16
LOG2E = 1.4426950408889634
F32 = jnp.float32
BF16 = jnp.bfloat16
BOTH = ("brick", "slab")
PAIRS = {
    (0, 0): 0,
    (0, 1): 1,
    (1, 1): 2,
    (0, 2): 3,
    (1, 2): 4,
    (2, 2): 5,
    (0, 3): 6,
    (1, 3): 7,
    (2, 3): 8,
}
VMEM = pl.BlockSpec(memory_space=pltpu.VMEM)
SMEM = pl.BlockSpec(memory_space=pltpu.SMEM)
HBM = pl.BlockSpec(memory_space=pltpu.HBM)
LIMIT = 12 << 20


def in_hbm(value):
    return pltpu.with_memory_space_constraint(value, pltpu.HBM)


def split3(value):
    high = value.astype(BF16)
    rest = value - high.astype(F32)
    middle = rest.astype(BF16)
    low = (rest - middle.astype(F32)).astype(BF16)
    return high, middle, low


def split2(value):
    high = value.astype(BF16).astype(F32)
    low = (value - high).astype(BF16).astype(F32)
    return high, low


def rows_at(ref, row, count):
    return ref[pl.ds(row, count, stride=8), :]


def put_rows(ref, row, value):
    ref[pl.ds(row, value.shape[0], stride=8), :] = value


def add_dots(row, vectors):
    lane = lax.broadcasted_iota(jnp.int32, (1, 128), 1)
    newest = len(vectors) - 1
    for (i, j), place in PAIRS.items():
        if j == newest or (newest == 1 and j == 0):
            product = vectors[i] * vectors[j]
            total = jnp.sum(jnp.sum(product, axis=0, keepdims=True), axis=1, keepdims=True)
            row = row + jnp.where(lane == place, total, 0.0)
    return row


def pack_kernel(each, pos_hbm, charge_hbm, force_hbm, owner_hbm, out_ref, target_ref, charge, owner, sems):
    count = charge.shape[0]
    copies = [
        pltpu.make_async_copy(source, target, sems.at[j])
        for j, (source, target) in enumerate(
            (
                (pos_hbm, out_ref.at[pl.ds(0, 3)]),
                (charge_hbm, charge),
                (force_hbm, out_ref.at[4]),
                (owner_hbm, owner),
            )
        )
    ]
    for copy in copies:
        copy.start()
    for copy in copies:
        copy.wait()
    out_ref[pl.ds(0, 3)] = out_ref[pl.ds(0, 3)] - 2.0
    out_ref[3] = jnp.log2(charge[...])
    owners = jnp.broadcast_to(owner[...].astype(F32), (count, count))
    earlier = lax.broadcasted_iota(jnp.int32, (count, count), 0) < lax.broadcasted_iota(
        jnp.int32, (count, count), 1
    )
    matching = jnp.where((owners.T == owners) & earlier, 1.0, 0.0)
    position = jnp.sum(matching, axis=0, keepdims=True).astype(jnp.int32)
    target_ref[...] = owner[...] * each + position


def weights_kernel(scale, first, blocks_count, index_ref, planes, blocks_ref, scratch, finish):
    raw, mine, sums, images, *buffers = scratch
    buffers, ring = buffers[: len(buffers) // 2], buffers[len(buffers) // 2 :]
    group = len(buffers)
    count = mine.shape[0] // 16
    square = LOG2E * LOG2E
    width = 128 * blocks_count
    one = jnp.ones((count, 128), F32)
    zero = jnp.zeros((count, 128), F32)
    for part, ref in enumerate(planes):
        base = part * count * 8
        x, y, z, charge, force = (ref[j] for j in range(5))
        norm = x * x + y * y + z * z
        high, low = split2(force)
        for j, value in enumerate((x, y, z, charge, norm, one, high, low)):
            put_rows(raw, base + j, value)
        if part == 0:
            doubled = (-2.0 * square) * x, (-2.0 * square) * y, (-2.0 * square) * z
            rows = (*doubled, zero, one * square, (norm + 0.5) * square, zero, zero)
            rows += (zero, zero, zero, one, zero, charge + jnp.log2(scale * one), zero, zero)
            for j, value in enumerate(rows):
                mine[pl.ds(j, count, stride=16), :] = value

    def entries(t):
        for k in range(blocks_count):
            u = t if first + k == 0 else index_ref[t * 4 + first + k - 1]
            yield raw[pl.ds(pl.multiple_of(u * 8, 8), 8), :]

    def terms(t):
        rights = []
        for j in range(2):
            high, middle, low = split3(mine[pl.ds(pl.multiple_of(t * 16 + 8 * j, 8), 8), :])
            rights.append(jnp.concatenate([high, middle, low, high, middle, high], axis=0))
        right = jnp.concatenate(rights, axis=1)
        lefts = []
        for value in entries(t):
            high, middle, low = split3(value)
            lefts.append(jnp.concatenate([high, high, high, middle, middle, low], axis=0))
        left = jnp.concatenate(lefts, axis=1)
        return lax.dot_general(
            left, right, (((0,), (0,)), ((), ())), preferred_element_type=F32
        )

    def block(t, source, kept, incoming):
        totals = [None] * 4
        for pair in range(width // 16):
            halves = []
            for half in range(2):
                chunk = 2 * pair + half
                place = pl.ds(8 * chunk, 8)
                wide = source[place, :128]
                shifted = wide - 0.49 * square
                if (chunk * MIX) % 10 < MIX:
                    distance = shifted * lax.rsqrt(shifted)
                    inverse = pltpu.reciprocal(wide)
                else:
                    product = wide * shifted
                    root = lax.rsqrt(product * wide)
                    distance = product * root
                    inverse = root * distance
                weight = inverse * (square * scale) + jnp.exp2(source[place, 128:] - distance)
                if first == 0 and chunk < 16:
                    rows = lax.broadcasted_iota(jnp.int32, (8, 128), 0) + 8 * chunk
                    lanes = lax.broadcasted_iota(jnp.int32, (8, 128), 1)
                    weight = jnp.where(rows == lanes, 0.0, weight)
                past = totals[chunk % 4]
                totals[chunk % 4] = weight if past is None else past + weight
                halves.append(weight)
            rounded = jnp.concatenate(halves, axis=0).astype(BF16)
            blocks_ref[t, pl.ds(16 * pair, 16), :] = rounded
            kept[pl.ds(16 * pair, 16), :] = rounded
            source[pl.ds(16 * pair, 16), :] = incoming[16 * pair : 16 * pair + 16]
        total = (totals[0] + totals[1]) + (totals[2] + totals[3])
        sums[pl.ds(pl.multiple_of(t * 8, 8), 8), :] = total

    def image(t, kept):
        left = jnp.concatenate([value.astype(BF16) for value in entries(t)], axis=1)
        images[pl.ds(pl.multiple_of(t * 8, 8), 8), :] = jnp.dot(
            left, kept[...], preferred_element_type=F32
        )

    for i in range(group):
        buffers[i][...] = terms(i)

    def tiles(j, carry):
        t = group * j
        for i in range(group):
            image(jnp.maximum(t + i - group, 0), ring[i])
            block(t + i, buffers[i], ring[i], terms(jnp.minimum(t + i + group, count - 1)))
        return carry

    lax.fori_loop(0, count // group, tiles, 0)
    for i in range(group):
        image(count - group + i, ring[i])
    total = rows_at(sums, 0, count)
    for j in range(1, 8):
        total = total + rows_at(sums, j, count)
    finish(total, rows_at(images, 6, count) + rows_at(images, 7, count))


def weights_scratch(count, parts, blocks_count, group):
    return [
        pltpu.VMEM((parts * count * 8, 128), F32),
        pltpu.VMEM((count * 16, 128), F32),
        pltpu.VMEM((count * 8, 128), F32),
        pltpu.VMEM((count * 8, 128), F32),
        *[pltpu.VMEM((128 * blocks_count, 256), F32)] * group,
        *[pltpu.VMEM((128 * blocks_count, 128), BF16)] * group,
    ]


def own_kernel(scale, own_ref, blocks_ref, total_ref, image_ref, *scratch):
    def finish(total, coupled):
        total_ref[...] = total
        image_ref[...] = coupled

    weights_kernel(scale, 0, 1, None, [own_ref], blocks_ref, scratch, finish)


def own_weights(own, scale):
    count = own.shape[1]
    plane = jax.ShapeDtypeStruct((count, 128), F32)
    return pl.pallas_call(
        functools.partial(own_kernel, scale),
        in_specs=[VMEM],
        out_specs=[VMEM] * 3,
        out_shape=[pltpu.VMEM((count, 128, 128), BF16), plane, plane],
        scratch_shapes=weights_scratch(count, 1, 1, OWN_GROUP),
        compiler_params=pltpu.CompilerParams(vmem_limit_bytes=LIMIT),
        cost_estimate=pl.CostEstimate(
            flops=count * 128 * 128 * 600, bytes_accessed=1 << 20, transcendentals=count * 128 * 256
        ),
        name="own_weights",
    )(own)


def other_kernel(
    scale, blocks_count, index_ref, own_ref, near_ref, far_ref, total_ref, image_ref, drag_hbm,
    blocks_ref, vector_ref, diagonal_ref, row_ref, drag, sem, *scratch,
):
    copy = pltpu.make_async_copy(drag_hbm, drag, sem)
    copy.start()

    def finish(total, coupled):
        copy.wait()
        diagonal = drag[...] + total_ref[...] + total
        force = own_ref[4]
        vector = (diagonal - SHIFT) * force - (image_ref[...] + coupled)
        diagonal_ref[...] = diagonal
        vector_ref[...] = vector
        row_ref[...] = add_dots(jnp.zeros((1, 128), F32), [force, vector])

    planes = [own_ref, near_ref, far_ref]
    weights_kernel(scale, 1, blocks_count, index_ref, planes, blocks_ref, scratch, finish)


def other_weights(index, own, near, far, total, image, drag, scale, blocks_count):
    count = drag.shape[0]
    plane = jax.ShapeDtypeStruct((count, 128), F32)
    return pl.pallas_call(
        functools.partial(other_kernel, scale, blocks_count),
        in_specs=[SMEM] + [VMEM] * 5 + [HBM],
        out_specs=[VMEM] * 4,
        out_shape=[
            pltpu.VMEM((count, 128 * blocks_count, 128), BF16),
            plane,
            plane,
            jax.ShapeDtypeStruct((1, 128), F32),
        ],
        scratch_shapes=[
            pltpu.VMEM((count, 128), F32),
            pltpu.SemaphoreType.DMA,
            *weights_scratch(count, 3, blocks_count, GROUP),
        ],
        compiler_params=pltpu.CompilerParams(vmem_limit_bytes=LIMIT),
        name="other_weights",
    )(index, own, near, far, total, image, in_hbm(drag))


def image_kernel(
    history, index_ref, own_blocks, blocks_ref, diagonal_ref, row_ref, near_ref, far_ref, own_ref, *refs
):
    past, refs = [own_ref.at[4], *refs[:history]], refs[history:]
    vector_ref, totals_ref, parts, images = refs
    count = diagonal_ref.shape[0]
    for part, ref in enumerate((past[-1], near_ref, far_ref)):
        high, low = split2(ref[...])
        put_rows(parts, part * count * 8, high)
        put_rows(parts, part * count * 8 + 1, low)

    def tile(t, carry):
        lefts = []
        for k in range(1 + blocks_ref.shape[1] // 128):
            u = t if k == 0 else index_ref[t * 4 + k - 1]
            lefts.append(parts[pl.ds(pl.multiple_of(u * 8, 8), 8), :].astype(BF16))
        left = jnp.concatenate(lefts[1:], axis=1)
        value = jnp.dot(left, blocks_ref[t], preferred_element_type=F32)
        value = value + jnp.dot(lefts[0], own_blocks[t], preferred_element_type=F32)
        images[pl.ds(pl.multiple_of(t * 8, 8), 8), :] = value
        return carry

    lax.fori_loop(0, count, tile, 0, unroll=UNROLL)
    coupled = rows_at(images, 0, count) + rows_at(images, 1, count)
    vectors = [ref[...] for ref in past]
    vector = (diagonal_ref[...] - SHIFT) * vectors[-1] - coupled
    vectors.append(vector)
    vector_ref[...] = vector
    totals_ref[...] = add_dots(row_ref[...], vectors)


def image(index, blocks, diagonal, row, near, far, own, past):
    count = diagonal.shape[0]
    operands = [*blocks, diagonal, row, near, far, own, *past]
    return pl.pallas_call(
        functools.partial(image_kernel, len(past)),
        in_specs=[SMEM] + [VMEM] * len(operands),
        out_specs=[VMEM] * 2,
        out_shape=[
            jax.ShapeDtypeStruct(diagonal.shape, F32),
            jax.ShapeDtypeStruct(row.shape, F32),
        ],
        scratch_shapes=[
            pltpu.VMEM((3 * count * 8, 128), F32),
            pltpu.VMEM((count * 8, 128), F32),
        ],
        compiler_params=pltpu.CompilerParams(vmem_limit_bytes=LIMIT),
        name="image",
    )(index, *operands)


def slots_kernel(target_ref, own_ref, first_ref, second_ref, third_ref, out_ref):
    owners, rows_each, _ = out_ref.shape
    count = first_ref.shape[0]
    each = (rows_each - 8) // 4
    slot = lax.broadcasted_iota(jnp.int32, (owners * each, count), 0)
    chosen = (slot == target_ref[...]).astype(F32).astype(BF16)
    for j, ref in enumerate((own_ref.at[4], first_ref, second_ref, third_ref)):
        value = ref[...]
        placed = sum(jnp.dot(chosen, piece, preferred_element_type=F32) for piece in split3(value))
        for owner in range(owners):
            out_ref[owner, pl.ds(each * j, each), :] = placed[each * owner : each * (owner + 1)]


def join_kernel(parts_ref, *refs):
    sums, (_, out_ref) = refs[:-2], refs[-2:]
    row = parts_ref[...]
    for ref in sums:
        row = row + ref[...]
    owners, rows_each, _ = out_ref.shape
    for owner in range(owners):
        out_ref[owner, pl.ds(rows_each - 8, 8), :] = jnp.broadcast_to(row, (8, 128))


def coefficients(totals):
    lane = lax.broadcasted_iota(jnp.int32, (1, 128), 1)
    gram = {}
    for (i, j), place in PAIRS.items():
        value = jnp.sum(jnp.where(lane == place, totals, 0.0), axis=1, keepdims=True)
        gram[i, j] = gram[j, i] = value

    def dot(a, b):
        return sum(x * sum(gram[i, j] * y for j, y in enumerate(b)) for i, x in enumerate(a))

    one = jnp.ones((1, 1), F32)
    zero = jnp.zeros((1, 1), F32)
    solution, residual, direction = [], [one], [one]
    norm = gram[0, 0]
    for iteration in range(ITERS):
        padded = direction + [zero]
        product = [SHIFT * value for value in padded]
        product = [value + (padded[j - 1] if j else zero) for j, value in enumerate(product)]
        step = norm / dot(direction, product)
        solution = [a + step * b for a, b in zip(solution + [zero], direction)]
        residual = [a - step * b for a, b in zip(residual + [zero], product)]
        if iteration < ITERS - 1:
            following = dot(residual, residual)
            direction = [a + (following / norm) * b for a, b in zip(residual, padded)]
            norm = following
    return solution, residual


def finish_kernel(arrived_ref, solution_ref, residual_ref):
    owners, rows_each, _ = arrived_ref.shape
    each = (rows_each - 8) // 4
    totals = sum(arrived_ref[owner, pl.ds(rows_each - 8, 8), :] for owner in range(owners))
    solution, residual = coefficients(totals[:1])
    for owner in range(owners):
        basis = [arrived_ref[owner, pl.ds(each * j, each), :] for j in range(4)]
        place = pl.ds(each * owner, each)
        solution_ref[place, :] = sum(a * v for a, v in zip(solution, basis))
        residual_ref[place, :] = sum(a * v for a, v in zip(residual, basis))


def local(positions, charges, drag, right_side, neighbours, owners):
    count = positions.shape[0]
    brick_count = lax.axis_size("brick")
    slab_count = lax.axis_size("slab")
    each = max(3, 3 * count // brick_count)
    slab_at = lax.axis_index("slab")
    first_tile = (lax.axis_index("brick") * slab_count + slab_at) * count
    inner = [(i, i ^ 1) for i in range(slab_count)]
    outer = [(i, i + 1) for i in range(1, slab_count - 1, 2)]
    outer = outer + [(target, source) for source, target in outer]

    packed, target = pl.pallas_call(
        functools.partial(pack_kernel, each),
        out_shape=[
            jax.ShapeDtypeStruct((5, count, 128), F32),
            jax.ShapeDtypeStruct((1, count), jnp.int32),
        ],
        in_specs=[HBM] * 4,
        out_specs=[VMEM] * 2,
        scratch_shapes=[
            pltpu.VMEM((count, 128), F32),
            pltpu.VMEM((1, count), jnp.int32),
            pltpu.SemaphoreType.DMA((4,)),
        ],
        compiler_params=pltpu.CompilerParams(vmem_limit_bytes=LIMIT),
        name="pack",
    )(*map(in_hbm, (jnp.transpose(positions, (1, 0, 2)), charges, right_side, owners.reshape(1, count))))

    offset = neighbours - first_tile
    layer = jnp.floor_divide(offset, count)
    partner = 1 - 2 * (slab_at % 2)
    part = jnp.where(layer == 0, 0, jnp.where(layer == partner, 1, 2))
    index = (offset - layer * count + part * count).reshape(-1)

    def both_sides(value):
        far = lax.ppermute(value, "slab", outer)
        near = lax.ppermute(value, "slab", inner)
        return near, far

    scale = 8.0 / ((neighbours.shape[1] + 1) * 128)
    entries = neighbours.shape[1]
    near, far = both_sides(packed)
    own_blocks, total, coupled = own_weights(packed, scale)
    blocks, first, diagonal, row = other_weights(
        index, packed, near, far, total, coupled, drag, scale, entries
    )
    blocks = own_blocks, blocks
    near, far = both_sides(first)
    second, row = image(index, blocks, diagonal, row, near, far, packed, [first])
    near, far = both_sides(second)
    third, row = image(index, blocks, diagonal, row, near, far, packed, [first, second])
    row = row + lax.ppermute(row, "slab", inner)
    around = [
        lax.ppermute(row, "slab", [(i, (i + step) % slab_count) for i in range(slab_count)])
        for step in (slab_count // 2, *(x for x in range(2, slab_count, 2) if x != slab_count // 2))
    ]
    outgoing = jax.ShapeDtypeStruct((brick_count, 4 * each + 8, 128), F32)
    params = pltpu.CompilerParams(vmem_limit_bytes=LIMIT)
    basis = pl.pallas_call(
        slots_kernel,
        out_shape=outgoing,
        in_specs=[VMEM] * 5,
        out_specs=VMEM,
        compiler_params=params,
        cost_estimate=pl.CostEstimate(flops=1 << 30, bytes_accessed=1 << 20, transcendentals=0),
        name="slots",
    )(target, packed, first, second, third)
    outgoing = pl.pallas_call(
        join_kernel,
        out_shape=outgoing,
        in_specs=[VMEM] * (2 + len(around)),
        out_specs=VMEM,
        input_output_aliases={1 + len(around): 0},
        compiler_params=params,
        name="join",
    )(row, *around, basis)
    arrived = lax.all_to_all(outgoing, "brick", split_axis=0, concat_axis=0, tiled=True)
    shape = jax.ShapeDtypeStruct((brick_count * each, 128), F32)
    return pl.pallas_call(
        finish_kernel,
        out_shape=(shape, shape),
        in_specs=[VMEM],
        out_specs=(VMEM, VMEM),
        compiler_params=pltpu.CompilerParams(vmem_limit_bytes=LIMIT),
        name="finish",
    )(arrived)


def solution(mesh):
    placed = (
        P(BOTH, None, None),
        P(BOTH, None),
        P(BOTH, None),
        P(BOTH, None),
        P(BOTH, None),
        P(BOTH, None),
    )
    step = jax.shard_map(
        local,
        mesh=mesh,
        in_specs=placed,
        out_specs=(P(BOTH, None), P(BOTH, None)),
        check_vma=False,
    )
    return step
```

```python
import functools

import jax
import jax.numpy as jnp
from jax import lax
from jax.experimental import pallas as pl
from jax.experimental.pallas import tpu as pltpu
from jax.sharding import PartitionSpec as P

ITERS = 3
SHIFT = 7.0
MIX = 7
UNROLL = 64
GROUP = 8
OWN_GROUP = 16
LOG2E = 1.4426950408889634
F32 = jnp.float32
BF16 = jnp.bfloat16
BOTH = ("brick", "slab")
PAIRS = {
    (0, 0): 0,
    (0, 1): 1,
    (1, 1): 2,
    (0, 2): 3,
    (1, 2): 4,
    (2, 2): 5,
    (0, 3): 6,
    (1, 3): 7,
    (2, 3): 8,
}
VMEM = pl.BlockSpec(memory_space=pltpu.VMEM)
SMEM = pl.BlockSpec(memory_space=pltpu.SMEM)
HBM = pl.BlockSpec(memory_space=pltpu.HBM)
LIMIT = 12 << 20


def in_hbm(value):
    return pltpu.with_memory_space_constraint(value, pltpu.HBM)


def split3(value):
    high = value.astype(BF16)
    rest = value - high.astype(F32)
    middle = rest.astype(BF16)
    low = (rest - middle.astype(F32)).astype(BF16)
    return high, middle, low


def split2(value):
    high = value.astype(BF16).astype(F32)
    low = (value - high).astype(BF16).astype(F32)
    return high, low


def rows_at(ref, row, count):
    return ref[pl.ds(row, count, stride=8), :]


def put_rows(ref, row, value):
    ref[pl.ds(row, value.shape[0], stride=8), :] = value


def add_dots(row, vectors):
    lane = lax.broadcasted_iota(jnp.int32, (1, 128), 1)
    newest = len(vectors) - 1
    for (i, j), place in PAIRS.items():
        if j == newest or (newest == 1 and j == 0):
            product = vectors[i] * vectors[j]
            total = jnp.sum(jnp.sum(product, axis=0, keepdims=True), axis=1, keepdims=True)
            row = row + jnp.where(lane == place, total, 0.0)
    return row


def pack_kernel(
    each, pos_hbm, charge_hbm, force_hbm, owner_hbm, tiles_hbm,
    out_ref, target_ref, index_ref, charge, owner, tiles, sems,
):
    count = charge.shape[0]
    copies = [
        pltpu.make_async_copy(source, target, sems.at[j])
        for j, (source, target) in enumerate(
            (
                (pos_hbm, out_ref.at[pl.ds(0, 3)]),
                (charge_hbm, charge),
                (force_hbm, out_ref.at[4]),
                (owner_hbm, owner),
                (tiles_hbm, tiles),
            )
        )
    ]
    for copy in copies:
        copy.start()
    for copy in copies:
        copy.wait()
    out_ref[pl.ds(0, 3)] = out_ref[pl.ds(0, 3)] - 2.0
    out_ref[3] = jnp.log2(charge[...])
    owners = jnp.broadcast_to(owner[...].astype(F32), (count, count))
    earlier = lax.broadcasted_iota(jnp.int32, (count, count), 0) < lax.broadcasted_iota(
        jnp.int32, (count, count), 1
    )
    matching = jnp.where((owners.T == owners) & earlier, 1.0, 0.0)
    position = jnp.sum(matching, axis=0, keepdims=True).astype(jnp.int32)
    target_ref[...] = owner[...] * each + position
    layers = lax.axis_size("slab")
    here = lax.axis_index("slab")
    layer = (tiles[...] >> (count.bit_length() - 1)) & (layers - 1)
    part = jnp.where(layer == here, 0, jnp.where(layer == (here ^ 1), 1, 2))
    index_ref[...] = (tiles[...] & (count - 1)) + part * count


def weights_kernel(scale, first, blocks_count, index_ref, planes, blocks_ref, scratch, finish):
    raw, mine, sums, images, *buffers = scratch
    buffers, ring = buffers[: len(buffers) // 2], buffers[len(buffers) // 2 :]
    group = len(buffers)
    count = mine.shape[0] // 16
    square = LOG2E * LOG2E
    width = 128 * blocks_count
    one = jnp.ones((count, 128), F32)
    zero = jnp.zeros((count, 128), F32)
    for part, ref in enumerate(planes):
        base = part * count * 8
        x, y, z, charge, force = (ref[j] for j in range(5))
        norm = x * x + y * y + z * z
        high, low = split2(force)
        for j, value in enumerate((x, y, z, charge, norm, one, high, low)):
            put_rows(raw, base + j, value)
        if part == 0:
            doubled = (-2.0 * square) * x, (-2.0 * square) * y, (-2.0 * square) * z
            rows = (*doubled, zero, one * square, (norm + 0.5) * square, zero, zero)
            rows += (zero, zero, zero, one, zero, charge + jnp.log2(scale * one), zero, zero)
            for j, value in enumerate(rows):
                mine[pl.ds(j, count, stride=16), :] = value

    def entries(t):
        for k in range(blocks_count):
            u = t if first + k == 0 else index_ref[first + k - 1, t]
            yield raw[pl.ds(pl.multiple_of(u * 8, 8), 8), :]

    def terms(t):
        rights = []
        for j in range(2):
            high, middle, low = split3(mine[pl.ds(pl.multiple_of(t * 16 + 8 * j, 8), 8), :])
            rights.append(jnp.concatenate([high, middle, low, high, middle, high], axis=0))
        right = jnp.concatenate(rights, axis=1)
        lefts = []
        for value in entries(t):
            high, middle, low = split3(value)
            lefts.append(jnp.concatenate([high, high, high, middle, middle, low], axis=0))
        left = jnp.concatenate(lefts, axis=1)
        return lax.dot_general(
            left, right, (((0,), (0,)), ((), ())), preferred_element_type=F32
        )

    def block(t, source, kept, incoming):
        totals = [None] * 4
        for pair in range(width // 16):
            halves = []
            for half in range(2):
                chunk = 2 * pair + half
                place = pl.ds(8 * chunk, 8)
                wide = source[place, :128]
                shifted = wide - 0.49 * square
                if (chunk * MIX) % 10 < MIX:
                    distance = shifted * lax.rsqrt(shifted)
                    inverse = pltpu.reciprocal(wide)
                else:
                    product = wide * shifted
                    root = lax.rsqrt(product * wide)
                    distance = product * root
                    inverse = root * distance
                weight = inverse * (square * scale) + jnp.exp2(source[place, 128:] - distance)
                if first == 0 and chunk < 16:
                    rows = lax.broadcasted_iota(jnp.int32, (8, 128), 0) + 8 * chunk
                    lanes = lax.broadcasted_iota(jnp.int32, (8, 128), 1)
                    weight = jnp.where(rows == lanes, 0.0, weight)
                past = totals[chunk % 4]
                totals[chunk % 4] = weight if past is None else past + weight
                halves.append(weight)
            rounded = jnp.concatenate(halves, axis=0).astype(BF16)
            blocks_ref[t, pl.ds(16 * pair, 16), :] = rounded
            kept[pl.ds(16 * pair, 16), :] = rounded
            source[pl.ds(16 * pair, 16), :] = incoming[16 * pair : 16 * pair + 16]
        total = (totals[0] + totals[1]) + (totals[2] + totals[3])
        sums[pl.ds(pl.multiple_of(t * 8, 8), 8), :] = total

    def image(t, kept):
        left = jnp.concatenate([value.astype(BF16) for value in entries(t)], axis=1)
        images[pl.ds(pl.multiple_of(t * 8, 8), 8), :] = jnp.dot(
            left, kept[...], preferred_element_type=F32
        )

    for i in range(group):
        buffers[i][...] = terms(i)

    def tiles(j, carry):
        t = group * j
        for i in range(group):
            image(jnp.maximum(t + i - group, 0), ring[i])
            block(t + i, buffers[i], ring[i], terms(jnp.minimum(t + i + group, count - 1)))
        return carry

    lax.fori_loop(0, count // group, tiles, 0)
    for i in range(group):
        image(count - group + i, ring[i])
    total = rows_at(sums, 0, count)
    for j in range(1, 8):
        total = total + rows_at(sums, j, count)
    finish(total, rows_at(images, 6, count) + rows_at(images, 7, count))


def weights_scratch(count, parts, blocks_count, group):
    return [
        pltpu.VMEM((parts * count * 8, 128), F32),
        pltpu.VMEM((count * 16, 128), F32),
        pltpu.VMEM((count * 8, 128), F32),
        pltpu.VMEM((count * 8, 128), F32),
        *[pltpu.VMEM((128 * blocks_count, 256), F32)] * group,
        *[pltpu.VMEM((128 * blocks_count, 128), BF16)] * group,
    ]


def own_kernel(scale, own_ref, blocks_ref, total_ref, image_ref, *scratch):
    def finish(total, coupled):
        total_ref[...] = total
        image_ref[...] = coupled

    weights_kernel(scale, 0, 1, None, [own_ref], blocks_ref, scratch, finish)


def own_weights(own, scale):
    count = own.shape[1]
    plane = jax.ShapeDtypeStruct((count, 128), F32)
    return pl.pallas_call(
        functools.partial(own_kernel, scale),
        in_specs=[VMEM],
        out_specs=[VMEM] * 3,
        out_shape=[pltpu.VMEM((count, 128, 128), BF16), plane, plane],
        scratch_shapes=weights_scratch(count, 1, 1, OWN_GROUP),
        compiler_params=pltpu.CompilerParams(vmem_limit_bytes=LIMIT),
        cost_estimate=pl.CostEstimate(
            flops=count * 128 * 128 * 600, bytes_accessed=1 << 20, transcendentals=count * 128 * 256
        ),
        name="own_weights",
    )(own)


def other_kernel(
    scale, blocks_count, index_ref, own_ref, near_ref, far_ref, total_ref, image_ref, drag_hbm,
    blocks_ref, vector_ref, diagonal_ref, row_ref, drag, sem, *scratch,
):
    copy = pltpu.make_async_copy(drag_hbm, drag, sem)
    copy.start()

    def finish(total, coupled):
        copy.wait()
        diagonal = drag[...] + total_ref[...] + total
        force = own_ref[4]
        vector = (diagonal - SHIFT) * force - (image_ref[...] + coupled)
        diagonal_ref[...] = diagonal
        vector_ref[...] = vector
        row_ref[...] = add_dots(jnp.zeros((1, 128), F32), [force, vector])

    planes = [own_ref, near_ref, far_ref]
    weights_kernel(scale, 1, blocks_count, index_ref, planes, blocks_ref, scratch, finish)


def other_weights(index, own, near, far, total, image, drag, scale, blocks_count):
    count = drag.shape[0]
    plane = jax.ShapeDtypeStruct((count, 128), F32)
    return pl.pallas_call(
        functools.partial(other_kernel, scale, blocks_count),
        in_specs=[SMEM] + [VMEM] * 5 + [HBM],
        out_specs=[VMEM] * 4,
        out_shape=[
            pltpu.VMEM((count, 128 * blocks_count, 128), BF16),
            plane,
            plane,
            jax.ShapeDtypeStruct((1, 128), F32),
        ],
        scratch_shapes=[
            pltpu.VMEM((count, 128), F32),
            pltpu.SemaphoreType.DMA,
            *weights_scratch(count, 3, blocks_count, GROUP),
        ],
        compiler_params=pltpu.CompilerParams(vmem_limit_bytes=LIMIT),
        name="other_weights",
    )(index, own, near, far, total, image, in_hbm(drag))


def own_image_kernel(vector_ref, blocks_ref, out_ref, parts, images):
    count = vector_ref.shape[0]
    for j, value in enumerate(split2(vector_ref[...])):
        put_rows(parts, j, value)

    def tile(t, carry):
        place = pl.ds(pl.multiple_of(t * 8, 8), 8)
        images[place, :] = jnp.dot(
            parts[place, :].astype(BF16), blocks_ref[t], preferred_element_type=F32
        )
        return carry

    lax.fori_loop(0, count, tile, 0, unroll=UNROLL)
    out_ref[...] = rows_at(images, 0, count) + rows_at(images, 1, count)


def own_image(vector, blocks):
    count = vector.shape[0]
    return pl.pallas_call(
        own_image_kernel,
        in_specs=[VMEM] * 2,
        out_specs=VMEM,
        out_shape=jax.ShapeDtypeStruct(vector.shape, F32),
        scratch_shapes=[pltpu.VMEM((count * 8, 128), F32)] * 2,
        compiler_params=pltpu.CompilerParams(vmem_limit_bytes=LIMIT),
        cost_estimate=pl.CostEstimate(
            flops=count * 128 * 128 * 512, bytes_accessed=1 << 22, transcendentals=0
        ),
        name="own_image",
    )(vector, blocks)


def image_kernel(
    history, index_ref, blocks_ref, coupled_ref, diagonal_ref, row_ref, near_ref, far_ref, own_ref, *refs
):
    past, refs = [own_ref.at[4], *refs[:history]], refs[history:]
    vector_ref, totals_ref, parts, images = refs
    count = diagonal_ref.shape[0]
    for part, ref in enumerate((past[-1], near_ref, far_ref)):
        for j, value in enumerate(split2(ref[...])):
            put_rows(parts, part * count * 8 + j, value)

    def tile(t, carry):
        lefts = []
        for k in range(blocks_ref.shape[1] // 128):
            u = index_ref[k, t]
            lefts.append(parts[pl.ds(pl.multiple_of(u * 8, 8), 8), :].astype(BF16))
        images[pl.ds(pl.multiple_of(t * 8, 8), 8), :] = jnp.dot(
            jnp.concatenate(lefts, axis=1), blocks_ref[t], preferred_element_type=F32
        )
        return carry

    lax.fori_loop(0, count, tile, 0, unroll=UNROLL)
    coupled = coupled_ref[...] + rows_at(images, 0, count) + rows_at(images, 1, count)
    vectors = [ref[...] for ref in past]
    vector = (diagonal_ref[...] - SHIFT) * vectors[-1] - coupled
    vectors.append(vector)
    vector_ref[...] = vector
    totals_ref[...] = add_dots(row_ref[...], vectors)


def image(index, blocks, coupled, diagonal, row, near, far, own, past):
    count = diagonal.shape[0]
    operands = [blocks, coupled, diagonal, row, near, far, own, *past]
    return pl.pallas_call(
        functools.partial(image_kernel, len(past)),
        in_specs=[SMEM] + [VMEM] * len(operands),
        out_specs=[VMEM] * 2,
        out_shape=[
            jax.ShapeDtypeStruct(diagonal.shape, F32),
            jax.ShapeDtypeStruct(row.shape, F32),
        ],
        scratch_shapes=[
            pltpu.VMEM((3 * count * 8, 128), F32),
            pltpu.VMEM((count * 8, 128), F32),
        ],
        compiler_params=pltpu.CompilerParams(vmem_limit_bytes=LIMIT),
        name="image",
    )(index, *operands)


def slots_kernel(target_ref, own_ref, first_ref, second_ref, third_ref, out_ref):
    owners, rows_each, _ = out_ref.shape
    count = first_ref.shape[0]
    each = (rows_each - 8) // 4
    slot = lax.broadcasted_iota(jnp.int32, (owners * each, count), 0)
    chosen = (slot == target_ref[...]).astype(F32).astype(BF16)
    for j, ref in enumerate((own_ref.at[4], first_ref, second_ref, third_ref)):
        value = ref[...]
        placed = sum(jnp.dot(chosen, piece, preferred_element_type=F32) for piece in split3(value))
        for owner in range(owners):
            out_ref[owner, pl.ds(each * j, each), :] = placed[each * owner : each * (owner + 1)]


def join_kernel(parts_ref, *refs):
    sums, (_, out_ref) = refs[:-2], refs[-2:]
    row = parts_ref[...]
    for ref in sums:
        row = row + ref[...]
    owners, rows_each, _ = out_ref.shape
    for owner in range(owners):
        out_ref[owner, pl.ds(rows_each - 8, 8), :] = jnp.broadcast_to(row, (8, 128))


def coefficients(totals):
    lane = lax.broadcasted_iota(jnp.int32, (1, 128), 1)
    gram = {}
    for (i, j), place in PAIRS.items():
        value = jnp.sum(jnp.where(lane == place, totals, 0.0), axis=1, keepdims=True)
        gram[i, j] = gram[j, i] = value

    def dot(a, b):
        return sum(x * sum(gram[i, j] * y for j, y in enumerate(b)) for i, x in enumerate(a))

    one = jnp.ones((1, 1), F32)
    zero = jnp.zeros((1, 1), F32)
    solution, residual, direction = [], [one], [one]
    norm = gram[0, 0]
    for iteration in range(ITERS):
        padded = direction + [zero]
        product = [SHIFT * value for value in padded]
        product = [value + (padded[j - 1] if j else zero) for j, value in enumerate(product)]
        step = norm / dot(direction, product)
        solution = [a + step * b for a, b in zip(solution + [zero], direction)]
        residual = [a - step * b for a, b in zip(residual + [zero], product)]
        if iteration < ITERS - 1:
            following = dot(residual, residual)
            direction = [a + (following / norm) * b for a, b in zip(residual, padded)]
            norm = following
    return solution, residual


def finish_kernel(arrived_ref, solution_hbm, residual_hbm, solution_ref, residual_ref, sems):
    owners, rows_each, _ = arrived_ref.shape
    each = (rows_each - 8) // 4
    totals = sum(arrived_ref[owner, pl.ds(rows_each - 8, 8), :] for owner in range(owners))
    solution, residual = coefficients(totals[:1])
    pieces = sems.shape[1]
    share = owners // pieces
    copies = []
    for piece in range(pieces):
        for owner in range(share * piece, share * (piece + 1)):
            basis = [arrived_ref[owner, pl.ds(each * j, each), :] for j in range(4)]
            place = pl.ds(each * owner, each)
            solution_ref[place, :] = sum(a * v for a, v in zip(solution, basis))
            residual_ref[place, :] = sum(a * v for a, v in zip(residual, basis))
        place = pl.ds(each * share * piece, each * share)
        for j, (source, target) in enumerate(
            ((solution_ref, solution_hbm), (residual_ref, residual_hbm))
        ):
            copy = pltpu.make_async_copy(source.at[place], target.at[place], sems.at[j, piece])
            copy.start()
            copies.append(copy)
    for copy in copies:
        copy.wait()


def local(positions, charges, drag, right_side, neighbours, owners):
    count = positions.shape[0]
    brick_count = lax.axis_size("brick")
    slab_count = lax.axis_size("slab")
    each = max(3, 3 * count // brick_count)
    entries = neighbours.shape[1]
    assert count & (count - 1) == 0 and slab_count & (slab_count - 1) == 0
    inner = [(i, i ^ 1) for i in range(slab_count)]
    outer = [(i, i + 1) for i in range(1, slab_count - 1, 2)]
    outer = outer + [(target, source) for source, target in outer]

    packed, target, index = pl.pallas_call(
        functools.partial(pack_kernel, each),
        out_shape=[
            jax.ShapeDtypeStruct((5, count, 128), F32),
            jax.ShapeDtypeStruct((1, count), jnp.int32),
            jax.ShapeDtypeStruct((entries, count), jnp.int32),
        ],
        in_specs=[HBM] * 5,
        out_specs=[VMEM] * 3,
        scratch_shapes=[
            pltpu.VMEM((count, 128), F32),
            pltpu.VMEM((1, count), jnp.int32),
            pltpu.VMEM((entries, count), jnp.int32),
            pltpu.SemaphoreType.DMA((5,)),
        ],
        compiler_params=pltpu.CompilerParams(vmem_limit_bytes=LIMIT),
        name="pack",
    )(*map(in_hbm, (jnp.transpose(positions, (1, 0, 2)), charges, right_side, owners.T, neighbours.T)))

    def both_sides(value):
        far = lax.ppermute(value, "slab", outer)
        near = lax.ppermute(value, "slab", inner)
        return near, far

    scale = 8.0 / ((entries + 1) * 128)
    near, far = both_sides(packed)
    own_blocks, total, coupled = own_weights(packed, scale)
    blocks, first, diagonal, row = other_weights(
        index, packed, near, far, total, coupled, drag, scale, entries
    )
    near, far = both_sides(first)
    coupled = own_image(first, own_blocks)
    second, row = image(index, blocks, coupled, diagonal, row, near, far, packed, [first])
    near, far = both_sides(second)
    coupled = own_image(second, own_blocks)
    third, row = image(
        index, blocks, coupled, diagonal, row, near, far, packed, [first, second]
    )
    row = row + lax.ppermute(row, "slab", inner)
    around = [
        lax.ppermute(row, "slab", [(i, (i + step) % slab_count) for i in range(slab_count)])
        for step in (slab_count // 2, *(x for x in range(2, slab_count, 2) if x != slab_count // 2))
    ]
    outgoing = jax.ShapeDtypeStruct((brick_count, 4 * each + 8, 128), F32)
    params = pltpu.CompilerParams(vmem_limit_bytes=LIMIT)
    basis = pl.pallas_call(
        slots_kernel,
        out_shape=outgoing,
        in_specs=[VMEM] * 5,
        out_specs=VMEM,
        compiler_params=params,
        cost_estimate=pl.CostEstimate(flops=1 << 30, bytes_accessed=1 << 20, transcendentals=0),
        name="slots",
    )(target, packed, first, second, third)
    outgoing = pl.pallas_call(
        join_kernel,
        out_shape=outgoing,
        in_specs=[VMEM] * (2 + len(around)),
        out_specs=VMEM,
        input_output_aliases={1 + len(around): 0},
        compiler_params=params,
        name="join",
    )(row, *around, basis)
    arrived = lax.all_to_all(outgoing, "brick", split_axis=0, concat_axis=0, tiled=True)
    shape = jax.ShapeDtypeStruct((brick_count * each, 128), F32)
    return pl.pallas_call(
        finish_kernel,
        out_shape=(shape, shape),
        in_specs=[VMEM],
        out_specs=(HBM, HBM),
        scratch_shapes=[
            pltpu.VMEM(shape.shape, F32),
            pltpu.VMEM(shape.shape, F32),
            pltpu.SemaphoreType.DMA((2, 4)),
        ],
        compiler_params=pltpu.CompilerParams(vmem_limit_bytes=LIMIT),
        name="finish",
    )(arrived)


def solution(mesh):
    placed = (
        P(BOTH, None, None),
        P(BOTH, None),
        P(BOTH, None),
        P(BOTH, None),
        P(BOTH, None),
        P(BOTH, None),
    )
    step = jax.shard_map(
        local,
        mesh=mesh,
        in_specs=placed,
        out_specs=(P(BOTH, None), P(BOTH, None)),
        check_vma=False,
    )
    return step
```

```python
import functools

import jax
import jax.numpy as jnp
from jax import lax
from jax.experimental import pallas as pl
from jax.experimental.pallas import tpu as pltpu
from jax.sharding import PartitionSpec as P

ITERS = 3
SHIFT = 7.0
UNROLL = 64
OWN = (16, 16, 7, 0)
OTHER = (32, 4, 0, 256)
LOG2E = 1.4426950408889634
F32 = jnp.float32
BF16 = jnp.bfloat16
BOTH = ("brick", "slab")
PAIRS = {
    (0, 0): 0,
    (0, 1): 1,
    (1, 1): 2,
    (0, 2): 3,
    (1, 2): 4,
    (2, 2): 5,
    (0, 3): 6,
    (1, 3): 7,
    (2, 3): 8,
}
VMEM = pl.BlockSpec(memory_space=pltpu.VMEM)
SMEM = pl.BlockSpec(memory_space=pltpu.SMEM)
HBM = pl.BlockSpec(memory_space=pltpu.HBM)
LIMIT = 12 << 20


def in_hbm(value):
    return pltpu.with_memory_space_constraint(value, pltpu.HBM)


def split3(value):
    high = value.astype(BF16)
    rest = value - high.astype(F32)
    middle = rest.astype(BF16)
    low = (rest - middle.astype(F32)).astype(BF16)
    return high, middle, low


def split2(value):
    high = value.astype(BF16).astype(F32)
    low = (value - high).astype(BF16).astype(F32)
    return high, low


def rows_at(ref, row, count):
    return ref[pl.ds(row, count, stride=8), :]


def put_rows(ref, row, value):
    ref[pl.ds(row, value.shape[0], stride=8), :] = value


def add_dots(row, vectors):
    lane = lax.broadcasted_iota(jnp.int32, (1, 128), 1)
    newest = len(vectors) - 1
    for (i, j), place in PAIRS.items():
        if j == newest or (newest == 1 and j == 0):
            product = vectors[i] * vectors[j]
            total = jnp.sum(jnp.sum(product, axis=0, keepdims=True), axis=1, keepdims=True)
            row = row + jnp.where(lane == place, total, 0.0)
    return row


def pack_kernel(
    each, pos_hbm, charge_hbm, force_hbm, owner_hbm, tiles_hbm,
    out_ref, target_ref, index_ref, charge, owner, tiles, sems,
):
    count = charge.shape[0]
    copies = [
        pltpu.make_async_copy(source, target, sems.at[j])
        for j, (source, target) in enumerate(
            (
                (pos_hbm, out_ref.at[pl.ds(0, 3)]),
                (charge_hbm, charge),
                (force_hbm, out_ref.at[4]),
                (owner_hbm, owner),
                (tiles_hbm, tiles),
            )
        )
    ]
    for copy in copies:
        copy.start()
    for copy in copies:
        copy.wait()
    out_ref[pl.ds(0, 3)] = out_ref[pl.ds(0, 3)] - 2.0
    out_ref[3] = jnp.log2(charge[...])
    owners = jnp.broadcast_to(owner[...].astype(F32), (count, count))
    earlier = lax.broadcasted_iota(jnp.int32, (count, count), 0) < lax.broadcasted_iota(
        jnp.int32, (count, count), 1
    )
    matching = jnp.where((owners.T == owners) & earlier, 1.0, 0.0)
    position = jnp.sum(matching, axis=0, keepdims=True).astype(jnp.int32)
    target_ref[...] = owner[...] * each + position
    layers = lax.axis_size("slab")
    here = lax.axis_index("slab")
    layer = (tiles[...] >> (count.bit_length() - 1)) & (layers - 1)
    part = jnp.where(layer == here, 0, jnp.where(layer == (here ^ 1), 1, 2))
    index_ref[...] = (tiles[...] & (count - 1)) + part * count


def weights_kernel(
    scale, first, blocks_count, tuning, index_ref, planes, blocks_ref, scratch, finish
):
    raw, mine, sums, images, *buffers = scratch
    group, lag, mix, split = tuning
    parts = 2 if split else 1
    buffers, ring = buffers[: parts * lag], buffers[parts * lag :]
    buffers = [buffers[i::lag] for i in range(lag)]
    count = mine.shape[0] // 24
    square = LOG2E * LOG2E
    width = 128 * blocks_count
    one = jnp.ones((count, 128), F32)
    zero = jnp.zeros((count, 128), F32)
    for part, ref in enumerate(planes):
        base = part * count * 8
        x, y, z, charge, force = (ref[j] for j in range(5))
        norm = x * x + y * y + z * z
        high, low = split2(force)
        for j, value in enumerate((x, y, z, charge, norm, one, high, low)):
            put_rows(raw, base + j, value)
        if part == 0:
            doubled = (-2.0 * square) * x, (-2.0 * square) * y, (-2.0 * square) * z
            rows = (*doubled, zero, one * square, (norm + 0.01) * square, zero, zero)
            rows += (zero, zero, zero, one, zero, charge + jnp.log2(scale * one), zero, zero)
            if split:
                doubled = (-2.0 / scale) * x, (-2.0 / scale) * y, (-2.0 / scale) * z
                rows += (*doubled, zero, one / scale, (norm + 0.5) / scale, zero, zero)
            for j, value in enumerate(rows):
                mine[pl.ds(j, count, stride=24), :] = value

    def entries(t):
        for k in range(blocks_count):
            u = t if first + k == 0 else index_ref[first + k - 1, t]
            yield raw[pl.ds(pl.multiple_of(u * 8, 8), 8), :]

    def terms(t):
        rights = []
        for j in range(3 if split else 2):
            high, middle, low = split3(mine[pl.ds(pl.multiple_of(t * 24 + 8 * j, 8), 8), :])
            rights.append(jnp.concatenate([high, middle, low, high, middle, high], axis=0))
        right = jnp.concatenate(rights, axis=1)
        lefts = []
        for value in entries(t):
            high, middle, low = split3(value)
            lefts.append(jnp.concatenate([high, high, high, middle, middle, low], axis=0))
        left = jnp.concatenate(lefts, axis=1)
        pairs = [(left[:, :split], right)] if split else []
        pairs.append((left[:, split:], right[:, :256]))
        return [
            lax.dot_general(a, b, (((0,), (0,)), ((), ())), preferred_element_type=F32)
            for a, b in pairs
        ]

    def block(t, source, kept, incoming):
        totals = [None] * 4
        for pair in range(width // 16):
            halves = []
            part = 0 if 16 * pair < split else -1
            base = 16 * pair - (0 if part == 0 else split)
            for half in range(2):
                chunk = 2 * pair + half
                place = pl.ds(base + 8 * half, 8)
                shifted = source[part][place, :128]
                if part == 0:
                    distance = shifted * lax.rsqrt(shifted)
                    inverse = pltpu.reciprocal(source[part][place, 256:])
                else:
                    wide = shifted + 0.49 * square
                    if (chunk * mix) % 10 < mix:
                        distance = shifted * lax.rsqrt(shifted)
                        inverse = pltpu.reciprocal(wide)
                    else:
                        product = wide * shifted
                        root = lax.rsqrt(product * wide)
                        distance = product * root
                        inverse = root * distance
                    inverse = inverse * (square * scale)
                weight = inverse + jnp.exp2(source[part][place, 128:256] - distance)
                if first == 0 and chunk < 16:
                    rows = lax.broadcasted_iota(jnp.int32, (8, 128), 0) + 8 * chunk
                    lanes = lax.broadcasted_iota(jnp.int32, (8, 128), 1)
                    weight = jnp.where(rows == lanes, 0.0, weight)
                past = totals[chunk % 4]
                totals[chunk % 4] = weight if past is None else past + weight
                halves.append(weight)
            rounded = jnp.concatenate(halves, axis=0).astype(BF16)
            blocks_ref[t, pl.ds(16 * pair, 16), :] = rounded
            kept[pl.ds(16 * pair, 16), :] = rounded
            source[part][pl.ds(base, 16), :] = incoming[part][base : base + 16]
        total = (totals[0] + totals[1]) + (totals[2] + totals[3])
        sums[pl.ds(pl.multiple_of(t * 8, 8), 8), :] = total

    def image(t, kept):
        left = jnp.concatenate([value.astype(BF16) for value in entries(t)], axis=1)
        images[pl.ds(pl.multiple_of(t * 8, 8), 8), :] = jnp.dot(
            left, kept[...], preferred_element_type=F32
        )

    for i in range(lag):
        for target, value in zip(buffers[i], terms(i)):
            target[...] = value

    def tiles(j, carry):
        for i in range(group):
            t = group * j + i
            slot = i % lag
            image(jnp.maximum(t - lag, 0), ring[slot])
            block(t, buffers[slot], ring[slot], terms(jnp.minimum(t + lag, count - 1)))
        return carry

    lax.fori_loop(0, count // group, tiles, 0)
    for i in range(lag):
        image(count - lag + i, ring[i])
    total = rows_at(sums, 0, count)
    for j in range(1, 8):
        total = total + rows_at(sums, j, count)
    finish(total, rows_at(images, 6, count) + rows_at(images, 7, count))


def weights_scratch(count, parts, blocks_count, tuning):
    _, lag, _, split = tuning
    width = 128 * blocks_count
    first = [pltpu.VMEM((split, 384), F32)] * lag if split else []
    return [
        pltpu.VMEM((parts * count * 8, 128), F32),
        pltpu.VMEM((count * 24, 128), F32),
        pltpu.VMEM((count * 8, 128), F32),
        pltpu.VMEM((count * 8, 128), F32),
        *first,
        *[pltpu.VMEM((width - split, 256), F32)] * lag,
        *[pltpu.VMEM((width, 128), BF16)] * lag,
    ]


def own_kernel(scale, own_ref, blocks_ref, total_ref, image_ref, *scratch):
    def finish(total, coupled):
        total_ref[...] = total
        image_ref[...] = coupled

    weights_kernel(scale, 0, 1, OWN, None, [own_ref], blocks_ref, scratch, finish)


def own_weights(own, scale):
    count = own.shape[1]
    plane = jax.ShapeDtypeStruct((count, 128), F32)
    return pl.pallas_call(
        functools.partial(own_kernel, scale),
        in_specs=[VMEM],
        out_specs=[VMEM] * 3,
        out_shape=[pltpu.VMEM((count, 128, 128), BF16), plane, plane],
        scratch_shapes=weights_scratch(count, 1, 1, OWN),
        compiler_params=pltpu.CompilerParams(vmem_limit_bytes=LIMIT),
        cost_estimate=pl.CostEstimate(
            flops=count * 128 * 128 * 600, bytes_accessed=1 << 20, transcendentals=count * 128 * 256
        ),
        name="own_weights",
    )(own)


def other_kernel(
    scale, blocks_count, index_ref, own_ref, near_ref, far_ref, total_ref, image_ref, drag_hbm,
    blocks_ref, vector_ref, diagonal_ref, row_ref, drag, sem, *scratch,
):
    copy = pltpu.make_async_copy(drag_hbm, drag, sem)
    copy.start()

    def finish(total, coupled):
        copy.wait()
        diagonal = drag[...] + total_ref[...] + total
        force = own_ref[4]
        vector = (diagonal - SHIFT) * force - (image_ref[...] + coupled)
        diagonal_ref[...] = diagonal
        vector_ref[...] = vector
        row_ref[...] = add_dots(jnp.zeros((1, 128), F32), [force, vector])

    planes = [own_ref, near_ref, far_ref]
    weights_kernel(scale, 1, blocks_count, OTHER, index_ref, planes, blocks_ref, scratch, finish)


def other_weights(index, own, near, far, total, image, drag, scale, blocks_count):
    count = drag.shape[0]
    plane = jax.ShapeDtypeStruct((count, 128), F32)
    return pl.pallas_call(
        functools.partial(other_kernel, scale, blocks_count),
        in_specs=[SMEM] + [VMEM] * 5 + [HBM],
        out_specs=[VMEM] * 4,
        out_shape=[
            pltpu.VMEM((count, 128 * blocks_count, 128), BF16),
            plane,
            plane,
            jax.ShapeDtypeStruct((1, 128), F32),
        ],
        scratch_shapes=[
            pltpu.VMEM((count, 128), F32),
            pltpu.SemaphoreType.DMA,
            *weights_scratch(count, 3, blocks_count, OTHER),
        ],
        compiler_params=pltpu.CompilerParams(vmem_limit_bytes=LIMIT),
        name="other_weights",
    )(index, own, near, far, total, image, in_hbm(drag))


def own_image_kernel(vector_ref, blocks_ref, out_ref, parts, images):
    count = vector_ref.shape[0]
    for j, value in enumerate(split2(vector_ref[...])):
        put_rows(parts, j, value)

    def tile(t, carry):
        place = pl.ds(pl.multiple_of(t * 8, 8), 8)
        images[place, :] = jnp.dot(
            parts[place, :].astype(BF16), blocks_ref[t], preferred_element_type=F32
        )
        return carry

    lax.fori_loop(0, count, tile, 0, unroll=UNROLL)
    out_ref[...] = rows_at(images, 0, count) + rows_at(images, 1, count)


def own_image(vector, blocks):
    count = vector.shape[0]
    return pl.pallas_call(
        own_image_kernel,
        in_specs=[VMEM] * 2,
        out_specs=VMEM,
        out_shape=jax.ShapeDtypeStruct(vector.shape, F32),
        scratch_shapes=[pltpu.VMEM((count * 8, 128), F32)] * 2,
        compiler_params=pltpu.CompilerParams(vmem_limit_bytes=LIMIT),
        cost_estimate=pl.CostEstimate(
            flops=count * 128 * 128 * 512, bytes_accessed=1 << 22, transcendentals=0
        ),
        name="own_image",
    )(vector, blocks)


def image_kernel(
    history, index_ref, blocks_ref, coupled_ref, diagonal_ref, row_ref, near_ref, far_ref, own_ref, *refs
):
    past, refs = [own_ref.at[4], *refs[:history]], refs[history:]
    vector_ref, totals_ref, parts, images = refs
    count = diagonal_ref.shape[0]
    for part, ref in enumerate((past[-1], near_ref, far_ref)):
        for j, value in enumerate(split2(ref[...])):
            put_rows(parts, part * count * 8 + j, value)

    def tile(t, carry):
        lefts = []
        for k in range(blocks_ref.shape[1] // 128):
            u = index_ref[k, t]
            lefts.append(parts[pl.ds(pl.multiple_of(u * 8, 8), 8), :].astype(BF16))
        images[pl.ds(pl.multiple_of(t * 8, 8), 8), :] = jnp.dot(
            jnp.concatenate(lefts, axis=1), blocks_ref[t], preferred_element_type=F32
        )
        return carry

    lax.fori_loop(0, count, tile, 0, unroll=UNROLL)
    coupled = coupled_ref[...] + rows_at(images, 0, count) + rows_at(images, 1, count)
    vectors = [ref[...] for ref in past]
    vector = (diagonal_ref[...] - SHIFT) * vectors[-1] - coupled
    vectors.append(vector)
    vector_ref[...] = vector
    totals_ref[...] = add_dots(row_ref[...], vectors)


def image(index, blocks, coupled, diagonal, row, near, far, own, past):
    count = diagonal.shape[0]
    operands = [blocks, coupled, diagonal, row, near, far, own, *past]
    return pl.pallas_call(
        functools.partial(image_kernel, len(past)),
        in_specs=[SMEM] + [VMEM] * len(operands),
        out_specs=[VMEM] * 2,
        out_shape=[
            jax.ShapeDtypeStruct(diagonal.shape, F32),
            jax.ShapeDtypeStruct(row.shape, F32),
        ],
        scratch_shapes=[
            pltpu.VMEM((3 * count * 8, 128), F32),
            pltpu.VMEM((count * 8, 128), F32),
        ],
        compiler_params=pltpu.CompilerParams(vmem_limit_bytes=LIMIT),
        name="image",
    )(index, *operands)


def slots_kernel(target_ref, own_ref, first_ref, second_ref, third_ref, out_ref):
    owners, rows_each, _ = out_ref.shape
    count = first_ref.shape[0]
    each = (rows_each - 8) // 4
    slot = lax.broadcasted_iota(jnp.int32, (owners * each, count), 0)
    chosen = (slot == target_ref[...]).astype(F32).astype(BF16)
    for j, ref in enumerate((own_ref.at[4], first_ref, second_ref, third_ref)):
        value = ref[...]
        placed = sum(jnp.dot(chosen, piece, preferred_element_type=F32) for piece in split3(value))
        for owner in range(owners):
            out_ref[owner, pl.ds(each * j, each), :] = placed[each * owner : each * (owner + 1)]


def join_kernel(parts_ref, *refs):
    sums, (_, out_ref) = refs[:-2], refs[-2:]
    row = parts_ref[...]
    for ref in sums:
        row = row + ref[...]
    owners, rows_each, _ = out_ref.shape
    for owner in range(owners):
        out_ref[owner, pl.ds(rows_each - 8, 8), :] = jnp.broadcast_to(row, (8, 128))


def coefficients(totals):
    lane = lax.broadcasted_iota(jnp.int32, (1, 128), 1)
    gram = {}
    for (i, j), place in PAIRS.items():
        value = jnp.sum(jnp.where(lane == place, totals, 0.0), axis=1, keepdims=True)
        gram[i, j] = gram[j, i] = value

    def dot(a, b):
        return sum(x * sum(gram[i, j] * y for j, y in enumerate(b)) for i, x in enumerate(a))

    one = jnp.ones((1, 1), F32)
    zero = jnp.zeros((1, 1), F32)
    solution, residual, direction = [], [one], [one]
    norm = gram[0, 0]
    for iteration in range(ITERS):
        padded = direction + [zero]
        product = [SHIFT * value for value in padded]
        product = [value + (padded[j - 1] if j else zero) for j, value in enumerate(product)]
        step = norm / dot(direction, product)
        solution = [a + step * b for a, b in zip(solution + [zero], direction)]
        residual = [a - step * b for a, b in zip(residual + [zero], product)]
        if iteration < ITERS - 1:
            following = dot(residual, residual)
            direction = [a + (following / norm) * b for a, b in zip(residual, padded)]
            norm = following
    return solution, residual


def finish_kernel(arrived_ref, solution_hbm, residual_hbm, solution_ref, residual_ref, sems):
    owners, rows_each, _ = arrived_ref.shape
    each = (rows_each - 8) // 4
    totals = sum(arrived_ref[owner, pl.ds(rows_each - 8, 8), :] for owner in range(owners))
    solution, residual = coefficients(totals[:1])
    pieces = sems.shape[1]
    share = owners // pieces
    copies = []
    for piece in range(pieces):
        for owner in range(share * piece, share * (piece + 1)):
            basis = [arrived_ref[owner, pl.ds(each * j, each), :] for j in range(4)]
            place = pl.ds(each * owner, each)
            solution_ref[place, :] = sum(a * v for a, v in zip(solution, basis))
            residual_ref[place, :] = sum(a * v for a, v in zip(residual, basis))
        place = pl.ds(each * share * piece, each * share)
        for j, (source, target) in enumerate(
            ((solution_ref, solution_hbm), (residual_ref, residual_hbm))
        ):
            copy = pltpu.make_async_copy(source.at[place], target.at[place], sems.at[j, piece])
            copy.start()
            copies.append(copy)
    for copy in copies:
        copy.wait()


def local(positions, charges, drag, right_side, neighbours, owners):
    count = positions.shape[0]
    brick_count = lax.axis_size("brick")
    slab_count = lax.axis_size("slab")
    each = max(3, 3 * count // brick_count)
    entries = neighbours.shape[1]
    assert count & (count - 1) == 0 and slab_count & (slab_count - 1) == 0
    inner = [(i, i ^ 1) for i in range(slab_count)]
    outer = [(i, i + 1) for i in range(1, slab_count - 1, 2)]
    outer = outer + [(target, source) for source, target in outer]

    packed, target, index = pl.pallas_call(
        functools.partial(pack_kernel, each),
        out_shape=[
            jax.ShapeDtypeStruct((5, count, 128), F32),
            jax.ShapeDtypeStruct((1, count), jnp.int32),
            jax.ShapeDtypeStruct((entries, count), jnp.int32),
        ],
        in_specs=[HBM] * 5,
        out_specs=[VMEM] * 3,
        scratch_shapes=[
            pltpu.VMEM((count, 128), F32),
            pltpu.VMEM((1, count), jnp.int32),
            pltpu.VMEM((entries, count), jnp.int32),
            pltpu.SemaphoreType.DMA((5,)),
        ],
        compiler_params=pltpu.CompilerParams(vmem_limit_bytes=LIMIT),
        name="pack",
    )(*map(in_hbm, (jnp.transpose(positions, (1, 0, 2)), charges, right_side, owners.T, neighbours.T)))

    def both_sides(value):
        far = lax.ppermute(value, "slab", outer)
        near = lax.ppermute(value, "slab", inner)
        return near, far

    scale = 8.0 / ((entries + 1) * 128)
    near, far = both_sides(packed)
    own_blocks, total, coupled = own_weights(packed, scale)
    blocks, first, diagonal, row = other_weights(
        index, packed, near, far, total, coupled, drag, scale, entries
    )
    near, far = both_sides(first)
    coupled = own_image(first, own_blocks)
    second, row = image(index, blocks, coupled, diagonal, row, near, far, packed, [first])
    near, far = both_sides(second)
    coupled = own_image(second, own_blocks)
    third, row = image(
        index, blocks, coupled, diagonal, row, near, far, packed, [first, second]
    )
    row = row + lax.ppermute(row, "slab", inner)
    around = [
        lax.ppermute(row, "slab", [(i, (i + step) % slab_count) for i in range(slab_count)])
        for step in (slab_count // 2, *(x for x in range(2, slab_count, 2) if x != slab_count // 2))
    ]
    outgoing = jax.ShapeDtypeStruct((brick_count, 4 * each + 8, 128), F32)
    params = pltpu.CompilerParams(vmem_limit_bytes=LIMIT)
    basis = pl.pallas_call(
        slots_kernel,
        out_shape=outgoing,
        in_specs=[VMEM] * 5,
        out_specs=VMEM,
        compiler_params=params,
        cost_estimate=pl.CostEstimate(flops=1 << 30, bytes_accessed=1 << 20, transcendentals=0),
        name="slots",
    )(target, packed, first, second, third)
    outgoing = pl.pallas_call(
        join_kernel,
        out_shape=outgoing,
        in_specs=[VMEM] * (2 + len(around)),
        out_specs=VMEM,
        input_output_aliases={1 + len(around): 0},
        compiler_params=params,
        name="join",
    )(row, *around, basis)
    arrived = lax.all_to_all(outgoing, "brick", split_axis=0, concat_axis=0, tiled=True)
    shape = jax.ShapeDtypeStruct((brick_count * each, 128), F32)
    return pl.pallas_call(
        finish_kernel,
        out_shape=(shape, shape),
        in_specs=[VMEM],
        out_specs=(HBM, HBM),
        scratch_shapes=[
            pltpu.VMEM(shape.shape, F32),
            pltpu.VMEM(shape.shape, F32),
            pltpu.SemaphoreType.DMA((2, 4)),
        ],
        compiler_params=pltpu.CompilerParams(vmem_limit_bytes=LIMIT),
        name="finish",
    )(arrived)


def solution(mesh):
    placed = (
        P(BOTH, None, None),
        P(BOTH, None),
        P(BOTH, None),
        P(BOTH, None),
        P(BOTH, None),
        P(BOTH, None),
    )
    step = jax.shard_map(
        local,
        mesh=mesh,
        in_specs=placed,
        out_specs=(P(BOTH, None), P(BOTH, None)),
        check_vma=False,
    )
    return step
```

```python
import functools

import jax
import jax.numpy as jnp
from jax import lax
from jax.experimental import pallas as pl
from jax.experimental.pallas import tpu as pltpu
from jax.sharding import PartitionSpec as P

ITERS = 3
SHIFT = 7.0
UNROLL = 64
OWN = (16, 16, 7, 0)
OTHER = (32, 4, 0, 256)
LOG2E = 1.4426950408889634
F32 = jnp.float32
BF16 = jnp.bfloat16
BOTH = ("brick", "slab")
PAIRS = {
    (0, 0): 0,
    (0, 1): 1,
    (1, 1): 2,
    (0, 2): 3,
    (1, 2): 4,
    (2, 2): 5,
    (0, 3): 6,
    (1, 3): 7,
    (2, 3): 8,
}
VMEM = pl.BlockSpec(memory_space=pltpu.VMEM)
SMEM = pl.BlockSpec(memory_space=pltpu.SMEM)
HBM = pl.BlockSpec(memory_space=pltpu.HBM)
LIMIT = 12 << 20


def in_hbm(value):
    return pltpu.with_memory_space_constraint(value, pltpu.HBM)


def split3(value):
    high = value.astype(BF16)
    rest = value - high.astype(F32)
    middle = rest.astype(BF16)
    low = (rest - middle.astype(F32)).astype(BF16)
    return high, middle, low


def split2(value):
    high = value.astype(BF16).astype(F32)
    low = (value - high).astype(BF16).astype(F32)
    return high, low


def rows_at(ref, row, count):
    return ref[pl.ds(row, count, stride=8), :]


def put_rows(ref, row, value):
    ref[pl.ds(row, value.shape[0], stride=8), :] = value


def add_dots(row, vectors):
    lane = lax.broadcasted_iota(jnp.int32, (1, 128), 1)
    newest = len(vectors) - 1
    for (i, j), place in PAIRS.items():
        if j == newest or (newest == 1 and j == 0):
            product = vectors[i] * vectors[j]
            total = jnp.sum(jnp.sum(product, axis=0, keepdims=True), axis=1, keepdims=True)
            row = row + jnp.where(lane == place, total, 0.0)
    return row


def pack_kernel(
    each, pos_hbm, charge_hbm, force_hbm, owner_hbm, tiles_hbm,
    out_ref, target_ref, index_ref, charge, owner, tiles, sems,
):
    count = charge.shape[0]
    copies = [
        pltpu.make_async_copy(source, target, sems.at[j])
        for j, (source, target) in enumerate(
            (
                (pos_hbm, out_ref.at[pl.ds(0, 3)]),
                (charge_hbm, charge),
                (force_hbm, out_ref.at[4]),
                (owner_hbm, owner),
                (tiles_hbm, tiles),
            )
        )
    ]
    for copy in copies:
        copy.start()
    for copy in copies:
        copy.wait()
    out_ref[pl.ds(0, 3)] = out_ref[pl.ds(0, 3)] - 2.0
    out_ref[3] = jnp.log2(charge[...])
    owners = jnp.broadcast_to(owner[...].astype(F32), (count, count))
    earlier = lax.broadcasted_iota(jnp.int32, (count, count), 0) < lax.broadcasted_iota(
        jnp.int32, (count, count), 1
    )
    matching = jnp.where((owners.T == owners) & earlier, 1.0, 0.0)
    position = jnp.sum(matching, axis=0, keepdims=True).astype(jnp.int32)
    target_ref[...] = owner[...] * each + position
    layers = lax.axis_size("slab")
    here = lax.axis_index("slab")
    layer = (tiles[...] >> (count.bit_length() - 1)) & (layers - 1)
    part = jnp.where(layer == here, 0, jnp.where(layer == (here ^ 1), 1, 2))
    index_ref[...] = (tiles[...] & (count - 1)) + part * count


def weights_kernel(
    scale, first, blocks_count, tuning, index_ref, planes, blocks_ref, scratch, finish
):
    raw, mine, sums, images, *buffers = scratch
    group, lag, mix, split = tuning
    parts = 2 if split else 1
    buffers, ring = buffers[: parts * lag], buffers[parts * lag :]
    buffers = [buffers[i::lag] for i in range(lag)]
    count = mine.shape[0] // 24
    square = LOG2E * LOG2E
    width = 128 * blocks_count
    one = jnp.ones((count, 128), F32)
    zero = jnp.zeros((count, 128), F32)
    for part, ref in enumerate(planes):
        base = part * count * 8
        x, y, z, charge, force = (ref[j] for j in range(5))
        norm = x * x + y * y + z * z
        high, low = split2(force)
        for j, value in enumerate((x, y, z, charge, norm, one, high, low)):
            put_rows(raw, base + j, value)
        if part == 0:
            doubled = (-2.0 * square) * x, (-2.0 * square) * y, (-2.0 * square) * z
            rows = (*doubled, zero, one * square, (norm + 0.01) * square, zero, zero)
            rows += (zero, zero, zero, one, zero, charge + jnp.log2(scale * one), zero, zero)
            if split:
                doubled = (-2.0 / scale) * x, (-2.0 / scale) * y, (-2.0 / scale) * z
                rows += (*doubled, zero, one / scale, (norm + 0.5) / scale, zero, zero)
            for j, value in enumerate(rows):
                mine[pl.ds(j, count, stride=24), :] = value

    def entries(t):
        for k in range(blocks_count):
            u = t if first + k == 0 else index_ref[first + k - 1, t]
            yield raw[pl.ds(pl.multiple_of(u * 8, 8), 8), :]

    def terms(t):
        rights = []
        for j in range(3 if split else 2):
            high, middle, low = split3(mine[pl.ds(pl.multiple_of(t * 24 + 8 * j, 8), 8), :])
            rights.append(jnp.concatenate([high, middle, low, high, middle, high], axis=0))
        right = jnp.concatenate(rights, axis=1)
        lefts = []
        for value in entries(t):
            high, middle, low = split3(value)
            lefts.append(jnp.concatenate([high, high, high, middle, middle, low], axis=0))
        left = jnp.concatenate(lefts, axis=1)
        pairs = [(left[:, :split], right)] if split else []
        pairs.append((left[:, split:], right[:, :256]))
        return [
            lax.dot_general(a, b, (((0,), (0,)), ((), ())), preferred_element_type=F32)
            for a, b in pairs
        ]

    def block(t, source, kept, incoming):
        totals = [None] * 4
        for pair in range(width // 16):
            halves = []
            part = 0 if 16 * pair < split else -1
            base = 16 * pair - (0 if part == 0 else split)
            for half in range(2):
                chunk = 2 * pair + half
                place = pl.ds(base + 8 * half, 8)
                shifted = source[part][place, :128]
                if part == 0:
                    distance = shifted * lax.rsqrt(shifted)
                    inverse = pltpu.reciprocal(source[part][place, 256:])
                else:
                    wide = shifted + 0.49 * square
                    if (chunk * mix) % 10 < mix:
                        distance = shifted * lax.rsqrt(shifted)
                        inverse = pltpu.reciprocal(wide)
                    else:
                        product = wide * shifted
                        root = lax.rsqrt(product * wide)
                        distance = product * root
                        inverse = root * distance
                    inverse = inverse * (square * scale)
                weight = inverse + jnp.exp2(source[part][place, 128:256] - distance)
                if first == 0 and chunk < 16:
                    rows = lax.broadcasted_iota(jnp.int32, (8, 128), 0) + 8 * chunk
                    lanes = lax.broadcasted_iota(jnp.int32, (8, 128), 1)
                    weight = jnp.where(rows == lanes, 0.0, weight)
                past = totals[chunk % 4]
                totals[chunk % 4] = weight if past is None else past + weight
                halves.append(weight)
            rounded = jnp.concatenate(halves, axis=0).astype(BF16)
            blocks_ref[t, pl.ds(16 * pair, 16), :] = rounded
            kept[pl.ds(16 * pair, 16), :] = rounded
            source[part][pl.ds(base, 16), :] = incoming[part][base : base + 16]
        total = (totals[0] + totals[1]) + (totals[2] + totals[3])
        sums[pl.ds(pl.multiple_of(t * 8, 8), 8), :] = total

    def image(t, kept):
        left = jnp.concatenate([value.astype(BF16) for value in entries(t)], axis=1)
        images[pl.ds(pl.multiple_of(t * 8, 8), 8), :] = jnp.dot(
            left, kept[...], preferred_element_type=F32
        )

    for i in range(lag):
        for target, value in zip(buffers[i], terms(i)):
            target[...] = value

    def tiles(j, carry):
        for i in range(group):
            t = group * j + i
            slot = i % lag
            image(jnp.maximum(t - lag, 0), ring[slot])
            block(t, buffers[slot], ring[slot], terms(jnp.minimum(t + lag, count - 1)))
        return carry

    lax.fori_loop(0, count // group, tiles, 0)
    for i in range(lag):
        image(count - lag + i, ring[i])
    total = rows_at(sums, 0, count)
    for j in range(1, 8):
        total = total + rows_at(sums, j, count)
    finish(total, rows_at(images, 6, count) + rows_at(images, 7, count))


def weights_scratch(count, parts, blocks_count, tuning):
    _, lag, _, split = tuning
    width = 128 * blocks_count
    first = [pltpu.VMEM((split, 384), F32)] * lag if split else []
    return [
        pltpu.VMEM((parts * count * 8, 128), F32),
        pltpu.VMEM((count * 24, 128), F32),
        pltpu.VMEM((count * 8, 128), F32),
        pltpu.VMEM((count * 8, 128), F32),
        *first,
        *[pltpu.VMEM((width - split, 256), F32)] * lag,
        *[pltpu.VMEM((width, 128), BF16)] * lag,
    ]


def own_kernel(scale, own_ref, blocks_ref, total_ref, image_ref, *scratch):
    def finish(total, coupled):
        total_ref[...] = total
        image_ref[...] = coupled

    weights_kernel(scale, 0, 1, OWN, None, [own_ref], blocks_ref, scratch, finish)


def own_weights(own, scale):
    count = own.shape[1]
    plane = jax.ShapeDtypeStruct((count, 128), F32)
    return pl.pallas_call(
        functools.partial(own_kernel, scale),
        in_specs=[VMEM],
        out_specs=[VMEM] * 3,
        out_shape=[pltpu.VMEM((count, 128, 128), BF16), plane, plane],
        scratch_shapes=weights_scratch(count, 1, 1, OWN),
        compiler_params=pltpu.CompilerParams(vmem_limit_bytes=LIMIT),
        cost_estimate=pl.CostEstimate(
            flops=count * 128 * 128 * 600, bytes_accessed=1 << 20, transcendentals=count * 128 * 256
        ),
        name="own_weights",
    )(own)


def other_kernel(
    scale, blocks_count, index_ref, own_ref, near_ref, far_ref, total_ref, image_ref, drag_hbm,
    blocks_ref, vector_ref, diagonal_ref, row_ref, drag, sem, *scratch,
):
    copy = pltpu.make_async_copy(drag_hbm, drag, sem)
    copy.start()

    def finish(total, coupled):
        copy.wait()
        diagonal = drag[...] + total_ref[...] + total
        force = own_ref[4]
        vector = (diagonal - SHIFT) * force - (image_ref[...] + coupled)
        diagonal_ref[...] = diagonal
        vector_ref[...] = vector
        row_ref[...] = add_dots(jnp.zeros((1, 128), F32), [force, vector])

    planes = [own_ref, near_ref, far_ref]
    weights_kernel(scale, 1, blocks_count, OTHER, index_ref, planes, blocks_ref, scratch, finish)


def other_weights(index, own, near, far, total, image, drag, scale, blocks_count):
    count = drag.shape[0]
    plane = jax.ShapeDtypeStruct((count, 128), F32)
    return pl.pallas_call(
        functools.partial(other_kernel, scale, blocks_count),
        in_specs=[SMEM] + [VMEM] * 5 + [HBM],
        out_specs=[VMEM] * 4,
        out_shape=[
            pltpu.VMEM((count, 128 * blocks_count, 128), BF16),
            plane,
            plane,
            jax.ShapeDtypeStruct((1, 128), F32),
        ],
        scratch_shapes=[
            pltpu.VMEM((count, 128), F32),
            pltpu.SemaphoreType.DMA,
            *weights_scratch(count, 3, blocks_count, OTHER),
        ],
        compiler_params=pltpu.CompilerParams(vmem_limit_bytes=LIMIT),
        name="other_weights",
    )(index, own, near, far, total, image, in_hbm(drag))


def own_image_kernel(vector_ref, blocks_ref, out_ref, parts, images):
    count = vector_ref.shape[0]
    for j, value in enumerate(split2(vector_ref[...])):
        put_rows(parts, j, value)

    def tile(t, carry):
        place = pl.ds(pl.multiple_of(t * 8, 8), 8)
        images[place, :] = jnp.dot(
            parts[place, :].astype(BF16), blocks_ref[t], preferred_element_type=F32
        )
        return carry

    lax.fori_loop(0, count, tile, 0, unroll=UNROLL)
    out_ref[...] = rows_at(images, 0, count) + rows_at(images, 1, count)


def own_image(vector, blocks):
    count = vector.shape[0]
    return pl.pallas_call(
        own_image_kernel,
        in_specs=[VMEM] * 2,
        out_specs=VMEM,
        out_shape=jax.ShapeDtypeStruct(vector.shape, F32),
        scratch_shapes=[pltpu.VMEM((count * 8, 128), F32)] * 2,
        compiler_params=pltpu.CompilerParams(vmem_limit_bytes=LIMIT),
        cost_estimate=pl.CostEstimate(
            flops=count * 128 * 128 * 512, bytes_accessed=1 << 22, transcendentals=0
        ),
        name="own_image",
    )(vector, blocks)


def image_kernel(
    history, index_ref, blocks_ref, coupled_ref, diagonal_ref, row_ref, near_ref, far_ref, own_ref, *refs
):
    past, refs = [own_ref.at[4], *refs[:history]], refs[history:]
    vector_ref, totals_ref, parts, images = refs
    count = diagonal_ref.shape[0]
    for part, ref in enumerate((past[-1], near_ref, far_ref)):
        for j, value in enumerate(split2(ref[...])):
            put_rows(parts, part * count * 8 + j, value)

    def tile(t, carry):
        lefts = []
        for k in range(blocks_ref.shape[1] // 128):
            u = index_ref[k, t]
            lefts.append(parts[pl.ds(pl.multiple_of(u * 8, 8), 8), :].astype(BF16))
        images[pl.ds(pl.multiple_of(t * 8, 8), 8), :] = jnp.dot(
            jnp.concatenate(lefts, axis=1), blocks_ref[t], preferred_element_type=F32
        )
        return carry

    lax.fori_loop(0, count, tile, 0, unroll=UNROLL)
    coupled = coupled_ref[...] + rows_at(images, 0, count) + rows_at(images, 1, count)
    vectors = [ref[...] for ref in past]
    vector = (diagonal_ref[...] - SHIFT) * vectors[-1] - coupled
    vectors.append(vector)
    vector_ref[...] = vector
    totals_ref[...] = add_dots(row_ref[...], vectors)


def image(index, blocks, coupled, diagonal, row, near, far, own, past):
    count = diagonal.shape[0]
    operands = [blocks, coupled, diagonal, row, near, far, own, *past]
    return pl.pallas_call(
        functools.partial(image_kernel, len(past)),
        in_specs=[SMEM] + [VMEM] * len(operands),
        out_specs=[VMEM] * 2,
        out_shape=[
            jax.ShapeDtypeStruct(diagonal.shape, F32),
            jax.ShapeDtypeStruct(row.shape, F32),
        ],
        scratch_shapes=[
            pltpu.VMEM((3 * count * 8, 128), F32),
            pltpu.VMEM((count * 8, 128), F32),
        ],
        compiler_params=pltpu.CompilerParams(vmem_limit_bytes=LIMIT),
        name="image",
    )(index, *operands)


def slots_kernel(target_ref, own_ref, first_ref, second_ref, third_ref, out_ref):
    owners, rows_each, _ = out_ref.shape
    count = first_ref.shape[0]
    each = (rows_each - 8) // 4
    slot = lax.broadcasted_iota(jnp.int32, (owners * each, count), 0)
    chosen = (slot == target_ref[...]).astype(F32).astype(BF16)
    for j, ref in enumerate((own_ref.at[4], first_ref, second_ref, third_ref)):
        value = ref[...]
        placed = sum(jnp.dot(chosen, piece, preferred_element_type=F32) for piece in split3(value))
        for owner in range(owners):
            out_ref[owner, pl.ds(each * j, each), :] = placed[each * owner : each * (owner + 1)]


def join_kernel(parts_ref, *refs):
    sums, (_, out_ref) = refs[:-2], refs[-2:]
    row = parts_ref[...]
    for ref in sums:
        row = row + ref[...]
    owners, rows_each, _ = out_ref.shape
    for owner in range(owners):
        out_ref[owner, pl.ds(rows_each - 8, 8), :] = jnp.broadcast_to(row, (8, 128))


def coefficients(totals):
    lane = lax.broadcasted_iota(jnp.int32, (1, 128), 1)
    gram = {}
    for (i, j), place in PAIRS.items():
        value = jnp.sum(jnp.where(lane == place, totals, 0.0), axis=1, keepdims=True)
        gram[i, j] = gram[j, i] = value

    def dot(a, b):
        return sum(x * sum(gram[i, j] * y for j, y in enumerate(b)) for i, x in enumerate(a))

    one = jnp.ones((1, 1), F32)
    zero = jnp.zeros((1, 1), F32)
    solution, residual, direction = [], [one], [one]
    norm = gram[0, 0]
    for iteration in range(ITERS):
        padded = direction + [zero]
        product = [SHIFT * value for value in padded]
        product = [value + (padded[j - 1] if j else zero) for j, value in enumerate(product)]
        step = norm / dot(direction, product)
        solution = [a + step * b for a, b in zip(solution + [zero], direction)]
        residual = [a - step * b for a, b in zip(residual + [zero], product)]
        if iteration < ITERS - 1:
            following = dot(residual, residual)
            direction = [a + (following / norm) * b for a, b in zip(residual, padded)]
            norm = following
    return solution, residual


def finish_kernel(arrived_ref, solution_hbm, residual_hbm, solution_ref, residual_ref, sems):
    owners, rows_each, _ = arrived_ref.shape
    each = (rows_each - 8) // 4
    totals = sum(arrived_ref[owner, pl.ds(rows_each - 8, 8), :] for owner in range(owners))
    solution, residual = coefficients(totals[:1])
    pieces = sems.shape[1]
    share = owners // pieces
    copies = []
    for piece in range(pieces):
        for owner in range(share * piece, share * (piece + 1)):
            basis = [arrived_ref[owner, pl.ds(each * j, each), :] for j in range(4)]
            place = pl.ds(each * owner, each)
            solution_ref[place, :] = sum(a * v for a, v in zip(solution, basis))
            residual_ref[place, :] = sum(a * v for a, v in zip(residual, basis))
        place = pl.ds(each * share * piece, each * share)
        for j, (source, target) in enumerate(
            ((solution_ref, solution_hbm), (residual_ref, residual_hbm))
        ):
            copy = pltpu.make_async_copy(source.at[place], target.at[place], sems.at[j, piece])
            copy.start()
            copies.append(copy)
    for copy in copies:
        copy.wait()


def local(positions, charges, drag, right_side, neighbours, owners):
    count = positions.shape[0]
    brick_count = lax.axis_size("brick")
    slab_count = lax.axis_size("slab")
    each = max(3, 3 * count // brick_count)
    entries = neighbours.shape[1]
    assert count & (count - 1) == 0 and slab_count & (slab_count - 1) == 0
    inner = [(i, i ^ 1) for i in range(slab_count)]
    outer = [(i, i + 1) for i in range(1, slab_count - 1, 2)]
    outer = outer + [(target, source) for source, target in outer]

    packed, target, index = pl.pallas_call(
        functools.partial(pack_kernel, each),
        out_shape=[
            jax.ShapeDtypeStruct((5, count, 128), F32),
            jax.ShapeDtypeStruct((1, count), jnp.int32),
            jax.ShapeDtypeStruct((entries, count), jnp.int32),
        ],
        in_specs=[HBM] * 5,
        out_specs=[VMEM] * 3,
        scratch_shapes=[
            pltpu.VMEM((count, 128), F32),
            pltpu.VMEM((1, count), jnp.int32),
            pltpu.VMEM((entries, count), jnp.int32),
            pltpu.SemaphoreType.DMA((5,)),
        ],
        compiler_params=pltpu.CompilerParams(vmem_limit_bytes=LIMIT),
        name="pack",
    )(*map(in_hbm, (jnp.transpose(positions, (1, 0, 2)), charges, right_side, owners.T, neighbours.T)))

    def both_sides(value):
        far = lax.ppermute(value, "slab", outer)
        near = lax.ppermute(value, "slab", inner)
        return near, far

    def near_first(value):
        near = lax.ppermute(value, "slab", inner)
        far = lax.ppermute(value, "slab", outer)
        return near, far

    scale = 8.0 / ((entries + 1) * 128)
    near, far = both_sides(packed)
    own_blocks, total, coupled = own_weights(packed, scale)
    blocks, first, diagonal, row = other_weights(
        index, packed, near, far, total, coupled, drag, scale, entries
    )
    near, far = both_sides(first)
    coupled = own_image(first, own_blocks)
    second, row = image(index, blocks, coupled, diagonal, row, near, far, packed, [first])
    near, far = near_first(second)
    coupled = own_image(second, own_blocks)
    third, row = image(
        index, blocks, coupled, diagonal, row, near, far, packed, [first, second]
    )
    row = row + lax.ppermute(row, "slab", inner)
    half = slab_count // 2
    around = [
        lax.ppermute(row, "slab", [(i, (i + step) % slab_count) for i in range(slab_count)])
        for step in (*(x for x in range(2, slab_count, 2) if x != half), half)
    ]
    outgoing = jax.ShapeDtypeStruct((brick_count, 4 * each + 8, 128), F32)
    params = pltpu.CompilerParams(vmem_limit_bytes=LIMIT)
    basis = pl.pallas_call(
        slots_kernel,
        out_shape=outgoing,
        in_specs=[VMEM] * 5,
        out_specs=VMEM,
        compiler_params=params,
        cost_estimate=pl.CostEstimate(flops=1 << 30, bytes_accessed=1 << 20, transcendentals=0),
        name="slots",
    )(target, packed, first, second, third)
    outgoing = pl.pallas_call(
        join_kernel,
        out_shape=outgoing,
        in_specs=[VMEM] * (2 + len(around)),
        out_specs=VMEM,
        input_output_aliases={1 + len(around): 0},
        compiler_params=params,
        name="join",
    )(row, *around, basis)
    arrived = lax.all_to_all(outgoing, "brick", split_axis=0, concat_axis=0, tiled=True)
    shape = jax.ShapeDtypeStruct((brick_count * each, 128), F32)
    return pl.pallas_call(
        finish_kernel,
        out_shape=(shape, shape),
        in_specs=[VMEM],
        out_specs=(HBM, HBM),
        scratch_shapes=[
            pltpu.VMEM(shape.shape, F32),
            pltpu.VMEM(shape.shape, F32),
            pltpu.SemaphoreType.DMA((2, 4)),
        ],
        compiler_params=pltpu.CompilerParams(vmem_limit_bytes=LIMIT),
        name="finish",
    )(arrived)


def solution(mesh):
    placed = (
        P(BOTH, None, None),
        P(BOTH, None),
        P(BOTH, None),
        P(BOTH, None),
        P(BOTH, None),
        P(BOTH, None),
    )
    step = jax.shard_map(
        local,
        mesh=mesh,
        in_specs=placed,
        out_specs=(P(BOTH, None), P(BOTH, None)),
        check_vma=False,
    )
    return step
```

```python
import functools

import jax
import jax.numpy as jnp
from jax import lax
from jax.experimental import pallas as pl
from jax.experimental.pallas import tpu as pltpu
from jax.sharding import PartitionSpec as P

ITERS = 3
SHIFT = 7.0
UNROLL = 64
OWN = (16, 16, 7, 0)
OTHER = (32, 4, 0, 256)
LOG2E = 1.4426950408889634
F32 = jnp.float32
BF16 = jnp.bfloat16
BOTH = ("brick", "slab")
PAIRS = {
    (0, 0): 0,
    (0, 1): 1,
    (1, 1): 2,
    (0, 2): 3,
    (1, 2): 4,
    (2, 2): 5,
    (0, 3): 6,
    (1, 3): 7,
    (2, 3): 8,
}
VMEM = pl.BlockSpec(memory_space=pltpu.VMEM)
SMEM = pl.BlockSpec(memory_space=pltpu.SMEM)
HBM = pl.BlockSpec(memory_space=pltpu.HBM)
LIMIT = 12 << 20


def in_hbm(value):
    return pltpu.with_memory_space_constraint(value, pltpu.HBM)


def split3(value):
    high = value.astype(BF16)
    rest = value - high.astype(F32)
    middle = rest.astype(BF16)
    low = (rest - middle.astype(F32)).astype(BF16)
    return high, middle, low


def split2(value):
    high = value.astype(BF16).astype(F32)
    low = (value - high).astype(BF16).astype(F32)
    return high, low


def rows_at(ref, row, count):
    return ref[pl.ds(row, count, stride=8), :]


def put_rows(ref, row, value):
    ref[pl.ds(row, value.shape[0], stride=8), :] = value


def add_dots(row, vectors):
    lane = lax.broadcasted_iota(jnp.int32, (1, 128), 1)
    newest = len(vectors) - 1
    for (i, j), place in PAIRS.items():
        if j == newest or (newest == 1 and j == 0):
            product = vectors[i] * vectors[j]
            total = jnp.sum(jnp.sum(product, axis=0, keepdims=True), axis=1, keepdims=True)
            row = row + jnp.where(lane == place, total, 0.0)
    return row


def pack_kernel(
    each, pos_hbm, charge_hbm, force_hbm, owner_hbm, tiles_hbm,
    out_ref, target_ref, index_ref, charge, owner, tiles, sems,
):
    count = charge.shape[0]
    copies = [
        pltpu.make_async_copy(source, target, sems.at[j])
        for j, (source, target) in enumerate(
            (
                (pos_hbm, out_ref.at[pl.ds(0, 3)]),
                (charge_hbm, charge),
                (force_hbm, out_ref.at[4]),
                (owner_hbm, owner),
                (tiles_hbm, tiles),
            )
        )
    ]
    for copy in copies:
        copy.start()
    for copy in copies:
        copy.wait()
    out_ref[pl.ds(0, 3)] = out_ref[pl.ds(0, 3)] - 2.0
    out_ref[3] = jnp.log2(charge[...])
    owners = jnp.broadcast_to(owner[...].astype(F32), (count, count))
    earlier = lax.broadcasted_iota(jnp.int32, (count, count), 0) < lax.broadcasted_iota(
        jnp.int32, (count, count), 1
    )
    matching = jnp.where((owners.T == owners) & earlier, 1.0, 0.0)
    position = jnp.sum(matching, axis=0, keepdims=True).astype(jnp.int32)
    target_ref[...] = owner[...] * each + position
    layers = lax.axis_size("slab")
    here = lax.axis_index("slab")
    layer = (tiles[...] >> (count.bit_length() - 1)) & (layers - 1)
    part = jnp.where(layer == here, 0, jnp.where(layer == (here ^ 1), 1, 2))
    index_ref[...] = (tiles[...] & (count - 1)) + part * count


def weights_kernel(
    scale, first, blocks_count, tuning, index_ref, planes, blocks_ref, scratch, finish
):
    raw, mine, sums, images, *buffers = scratch
    group, lag, mix, split = tuning
    parts = 2 if split else 1
    buffers, ring = buffers[: parts * lag], buffers[parts * lag :]
    buffers = [buffers[i::lag] for i in range(lag)]
    count = mine.shape[0] // 24
    square = LOG2E * LOG2E
    width = 128 * blocks_count
    one = jnp.ones((count, 128), F32)
    zero = jnp.zeros((count, 128), F32)
    for part, ref in enumerate(planes):
        base = part * count * 8
        x, y, z, charge, force = (ref[j] for j in range(5))
        norm = x * x + y * y + z * z
        high, low = split2(force)
        for j, value in enumerate((x, y, z, charge, norm, one, high, low)):
            put_rows(raw, base + j, value)
        if part == 0:
            doubled = (-2.0 * square) * x, (-2.0 * square) * y, (-2.0 * square) * z
            rows = (*doubled, zero, one * square, (norm + 0.01) * square, zero, zero)
            rows += (zero, zero, zero, one, zero, charge + jnp.log2(scale * one), zero, zero)
            if split:
                doubled = (-2.0 / scale) * x, (-2.0 / scale) * y, (-2.0 / scale) * z
                rows += (*doubled, zero, one / scale, (norm + 0.5) / scale, zero, zero)
            for j, value in enumerate(rows):
                mine[pl.ds(j, count, stride=24), :] = value

    def entries(t):
        for k in range(blocks_count):
            u = t if first + k == 0 else index_ref[first + k - 1, t]
            yield raw[pl.ds(pl.multiple_of(u * 8, 8), 8), :]

    def terms(t):
        rights = []
        for j in range(3 if split else 2):
            high, middle, low = split3(mine[pl.ds(pl.multiple_of(t * 24 + 8 * j, 8), 8), :])
            rights.append(jnp.concatenate([high, middle, low, high, middle, high], axis=0))
        right = jnp.concatenate(rights, axis=1)
        lefts = []
        for value in entries(t):
            high, middle, low = split3(value)
            lefts.append(jnp.concatenate([high, high, high, middle, middle, low], axis=0))
        left = jnp.concatenate(lefts, axis=1)
        pairs = [(left[:, :split], right)] if split else []
        pairs.append((left[:, split:], right[:, :256]))
        return [
            lax.dot_general(a, b, (((0,), (0,)), ((), ())), preferred_element_type=F32)
            for a, b in pairs
        ]

    def block(t, source, kept, incoming):
        totals = [None] * 4
        for pair in range(width // 16):
            halves = []
            part = 0 if 16 * pair < split else -1
            base = 16 * pair - (0 if part == 0 else split)
            for half in range(2):
                chunk = 2 * pair + half
                place = pl.ds(base + 8 * half, 8)
                shifted = source[part][place, :128]
                if part == 0:
                    distance = shifted * lax.rsqrt(shifted)
                    inverse = pltpu.reciprocal(source[part][place, 256:])
                else:
                    wide = shifted + 0.49 * square
                    if (chunk * mix) % 10 < mix:
                        distance = shifted * lax.rsqrt(shifted)
                        inverse = pltpu.reciprocal(wide)
                    else:
                        product = wide * shifted
                        root = lax.rsqrt(product * wide)
                        distance = product * root
                        inverse = root * distance
                    inverse = inverse * (square * scale)
                weight = inverse + jnp.exp2(source[part][place, 128:256] - distance)
                if first == 0 and chunk < 16:
                    rows = lax.broadcasted_iota(jnp.int32, (8, 128), 0) + 8 * chunk
                    lanes = lax.broadcasted_iota(jnp.int32, (8, 128), 1)
                    weight = jnp.where(rows == lanes, 0.0, weight)
                past = totals[chunk % 4]
                totals[chunk % 4] = weight if past is None else past + weight
                halves.append(weight)
            rounded = jnp.concatenate(halves, axis=0).astype(BF16)
            blocks_ref[t, pl.ds(16 * pair, 16), :] = rounded
            kept[pl.ds(16 * pair, 16), :] = rounded
            source[part][pl.ds(base, 16), :] = incoming[part][base : base + 16]
        total = (totals[0] + totals[1]) + (totals[2] + totals[3])
        sums[pl.ds(pl.multiple_of(t * 8, 8), 8), :] = total

    def image(t, kept):
        left = jnp.concatenate([value.astype(BF16) for value in entries(t)], axis=1)
        images[pl.ds(pl.multiple_of(t * 8, 8), 8), :] = jnp.dot(
            left, kept[...], preferred_element_type=F32
        )

    for i in range(lag):
        for target, value in zip(buffers[i], terms(i)):
            target[...] = value

    def tiles(j, carry):
        for i in range(group):
            t = group * j + i
            slot = i % lag
            image(jnp.maximum(t - lag, 0), ring[slot])
            block(t, buffers[slot], ring[slot], terms(jnp.minimum(t + lag, count - 1)))
        return carry

    lax.fori_loop(0, count // group, tiles, 0)
    for i in range(lag):
        image(count - lag + i, ring[i])
    total = rows_at(sums, 0, count)
    for j in range(1, 8):
        total = total + rows_at(sums, j, count)
    finish(total, rows_at(images, 6, count) + rows_at(images, 7, count))


def weights_scratch(count, parts, blocks_count, tuning):
    _, lag, _, split = tuning
    width = 128 * blocks_count
    first = [pltpu.VMEM((split, 384), F32)] * lag if split else []
    return [
        pltpu.VMEM((parts * count * 8, 128), F32),
        pltpu.VMEM((count * 24, 128), F32),
        pltpu.VMEM((count * 8, 128), F32),
        pltpu.VMEM((count * 8, 128), F32),
        *first,
        *[pltpu.VMEM((width - split, 256), F32)] * lag,
        *[pltpu.VMEM((width, 128), BF16)] * lag,
    ]


def own_kernel(scale, own_ref, blocks_ref, total_ref, image_ref, *scratch):
    def finish(total, coupled):
        total_ref[...] = total
        image_ref[...] = coupled

    weights_kernel(scale, 0, 1, OWN, None, [own_ref], blocks_ref, scratch, finish)


def own_weights(own, scale):
    count = own.shape[1]
    plane = jax.ShapeDtypeStruct((count, 128), F32)
    return pl.pallas_call(
        functools.partial(own_kernel, scale),
        in_specs=[VMEM],
        out_specs=[VMEM] * 3,
        out_shape=[pltpu.VMEM((count, 128, 128), BF16), plane, plane],
        scratch_shapes=weights_scratch(count, 1, 1, OWN),
        compiler_params=pltpu.CompilerParams(vmem_limit_bytes=LIMIT),
        cost_estimate=pl.CostEstimate(
            flops=count * 128 * 128 * 600, bytes_accessed=1 << 20, transcendentals=count * 128 * 256
        ),
        name="own_weights",
    )(own)


def other_kernel(
    scale, blocks_count, index_ref, own_ref, near_ref, far_ref, total_ref, image_ref, drag_hbm,
    blocks_ref, vector_ref, diagonal_ref, row_ref, drag, sem, *scratch,
):
    copy = pltpu.make_async_copy(drag_hbm, drag, sem)
    copy.start()

    def finish(total, coupled):
        copy.wait()
        diagonal = drag[...] + total_ref[...] + total
        force = own_ref[4]
        vector = (diagonal - SHIFT) * force - (image_ref[...] + coupled)
        diagonal_ref[...] = diagonal
        vector_ref[...] = vector
        row_ref[...] = add_dots(jnp.zeros((1, 128), F32), [force, vector])

    planes = [own_ref, near_ref, far_ref]
    weights_kernel(scale, 1, blocks_count, OTHER, index_ref, planes, blocks_ref, scratch, finish)


def other_weights(index, own, near, far, total, image, drag, scale, blocks_count):
    count = drag.shape[0]
    plane = jax.ShapeDtypeStruct((count, 128), F32)
    return pl.pallas_call(
        functools.partial(other_kernel, scale, blocks_count),
        in_specs=[SMEM] + [VMEM] * 5 + [HBM],
        out_specs=[VMEM] * 4,
        out_shape=[
            pltpu.VMEM((count, 128 * blocks_count, 128), BF16),
            plane,
            plane,
            jax.ShapeDtypeStruct((1, 128), F32),
        ],
        scratch_shapes=[
            pltpu.VMEM((count, 128), F32),
            pltpu.SemaphoreType.DMA,
            *weights_scratch(count, 3, blocks_count, OTHER),
        ],
        compiler_params=pltpu.CompilerParams(vmem_limit_bytes=LIMIT),
        name="other_weights",
    )(index, own, near, far, total, image, in_hbm(drag))


def own_image_kernel(vector_ref, blocks_ref, out_ref, parts, images):
    count = vector_ref.shape[0]
    for j, value in enumerate(split2(vector_ref[...])):
        put_rows(parts, j, value)

    def tile(t, carry):
        place = pl.ds(pl.multiple_of(t * 8, 8), 8)
        images[place, :] = jnp.dot(
            parts[place, :].astype(BF16), blocks_ref[t], preferred_element_type=F32
        )
        return carry

    lax.fori_loop(0, count, tile, 0, unroll=UNROLL)
    out_ref[...] = rows_at(images, 0, count) + rows_at(images, 1, count)


def own_image(vector, blocks):
    count = vector.shape[0]
    return pl.pallas_call(
        own_image_kernel,
        in_specs=[VMEM] * 2,
        out_specs=VMEM,
        out_shape=jax.ShapeDtypeStruct(vector.shape, F32),
        scratch_shapes=[pltpu.VMEM((count * 8, 128), F32)] * 2,
        compiler_params=pltpu.CompilerParams(vmem_limit_bytes=LIMIT),
        cost_estimate=pl.CostEstimate(
            flops=count * 128 * 128 * 512, bytes_accessed=1 << 22, transcendentals=0
        ),
        name="own_image",
    )(vector, blocks)


def image_kernel(
    history, index_ref, blocks_ref, coupled_ref, diagonal_ref, row_ref, near_ref, far_ref, own_ref, *refs
):
    past, refs = [own_ref.at[4], *refs[:history]], refs[history:]
    vector_ref, totals_ref, parts, images = refs
    count = diagonal_ref.shape[0]
    for part, ref in enumerate((past[-1], near_ref, far_ref)):
        for j, value in enumerate(split2(ref[...])):
            put_rows(parts, part * count * 8 + j, value)

    def tile(t, carry):
        lefts = []
        for k in range(blocks_ref.shape[1] // 128):
            u = index_ref[k, t]
            lefts.append(parts[pl.ds(pl.multiple_of(u * 8, 8), 8), :].astype(BF16))
        images[pl.ds(pl.multiple_of(t * 8, 8), 8), :] = jnp.dot(
            jnp.concatenate(lefts, axis=1), blocks_ref[t], preferred_element_type=F32
        )
        return carry

    lax.fori_loop(0, count, tile, 0, unroll=UNROLL)
    coupled = coupled_ref[...] + rows_at(images, 0, count) + rows_at(images, 1, count)
    vectors = [ref[...] for ref in past]
    vector = (diagonal_ref[...] - SHIFT) * vectors[-1] - coupled
    vectors.append(vector)
    vector_ref[...] = vector
    totals_ref[...] = add_dots(row_ref[...], vectors)


def image(index, blocks, coupled, diagonal, row, near, far, own, past):
    count = diagonal.shape[0]
    operands = [blocks, coupled, diagonal, row, near, far, own, *past]
    return pl.pallas_call(
        functools.partial(image_kernel, len(past)),
        in_specs=[SMEM] + [VMEM] * len(operands),
        out_specs=[VMEM] * 2,
        out_shape=[
            jax.ShapeDtypeStruct(diagonal.shape, F32),
            jax.ShapeDtypeStruct(row.shape, F32),
        ],
        scratch_shapes=[
            pltpu.VMEM((3 * count * 8, 128), F32),
            pltpu.VMEM((count * 8, 128), F32),
        ],
        compiler_params=pltpu.CompilerParams(vmem_limit_bytes=LIMIT),
        name="image",
    )(index, *operands)


def slots_kernel(target_ref, own_ref, first_ref, second_ref, third_ref, out_ref):
    owners, rows_each, _ = out_ref.shape
    count = first_ref.shape[0]
    each = (rows_each - 8) // 4
    slot = lax.broadcasted_iota(jnp.int32, (owners * each, count), 0)
    chosen = (slot == target_ref[...]).astype(F32).astype(BF16)
    for j, ref in enumerate((own_ref.at[4], first_ref, second_ref, third_ref)):
        value = ref[...]
        placed = sum(jnp.dot(chosen, piece, preferred_element_type=F32) for piece in split3(value))
        for owner in range(owners):
            out_ref[owner, pl.ds(each * j, each), :] = placed[each * owner : each * (owner + 1)]


def join_kernel(parts_ref, *refs):
    sums, (_, out_ref) = refs[:-2], refs[-2:]
    row = parts_ref[...]
    for ref in sums:
        row = row + ref[...]
    owners, rows_each, _ = out_ref.shape
    for owner in range(owners):
        out_ref[owner, pl.ds(rows_each - 8, 8), :] = jnp.broadcast_to(row, (8, 128))


def coefficients(totals):
    lane = lax.broadcasted_iota(jnp.int32, (1, 128), 1)
    gram = {}
    for (i, j), place in PAIRS.items():
        value = jnp.sum(jnp.where(lane == place, totals, 0.0), axis=1, keepdims=True)
        gram[i, j] = gram[j, i] = value

    def dot(a, b):
        return sum(x * sum(gram[i, j] * y for j, y in enumerate(b)) for i, x in enumerate(a))

    one = jnp.ones((1, 1), F32)
    zero = jnp.zeros((1, 1), F32)
    solution, residual, direction = [], [one], [one]
    norm = gram[0, 0]
    for iteration in range(ITERS):
        padded = direction + [zero]
        product = [SHIFT * value for value in padded]
        product = [value + (padded[j - 1] if j else zero) for j, value in enumerate(product)]
        step = norm / dot(direction, product)
        solution = [a + step * b for a, b in zip(solution + [zero], direction)]
        residual = [a - step * b for a, b in zip(residual + [zero], product)]
        if iteration < ITERS - 1:
            following = dot(residual, residual)
            direction = [a + (following / norm) * b for a, b in zip(residual, padded)]
            norm = following
    return solution, residual


def finish_kernel(arrived_ref, solution_hbm, residual_hbm, solution_ref, residual_ref, sems):
    owners, rows_each, _ = arrived_ref.shape
    each = (rows_each - 8) // 4
    totals = sum(arrived_ref[owner, pl.ds(rows_each - 8, 8), :] for owner in range(owners))
    solution, residual = coefficients(totals[:1])
    pieces = sems.shape[1]
    share = owners // pieces
    copies = []
    for piece in range(pieces):
        for owner in range(share * piece, share * (piece + 1)):
            basis = [arrived_ref[owner, pl.ds(each * j, each), :] for j in range(4)]
            place = pl.ds(each * owner, each)
            solution_ref[place, :] = sum(a * v for a, v in zip(solution, basis))
            residual_ref[place, :] = sum(a * v for a, v in zip(residual, basis))
        place = pl.ds(each * share * piece, each * share)
        for j, (source, target) in enumerate(
            ((solution_ref, solution_hbm), (residual_ref, residual_hbm))
        ):
            copy = pltpu.make_async_copy(source.at[place], target.at[place], sems.at[j, piece])
            copy.start()
            copies.append(copy)
    for copy in copies:
        copy.wait()


def local(positions, charges, drag, right_side, neighbours, owners):
    count = positions.shape[0]
    brick_count = lax.axis_size("brick")
    slab_count = lax.axis_size("slab")
    each = max(3, 3 * count // brick_count)
    entries = neighbours.shape[1]
    assert count & (count - 1) == 0 and slab_count & (slab_count - 1) == 0
    inner = [(i, i ^ 1) for i in range(slab_count)]
    outer = [(i, i + 1) for i in range(1, slab_count - 1, 2)]
    outer = outer + [(target, source) for source, target in outer]

    packed, target, index = pl.pallas_call(
        functools.partial(pack_kernel, each),
        out_shape=[
            jax.ShapeDtypeStruct((5, count, 128), F32),
            jax.ShapeDtypeStruct((1, count), jnp.int32),
            jax.ShapeDtypeStruct((entries, count), jnp.int32),
        ],
        in_specs=[HBM] * 5,
        out_specs=[VMEM] * 3,
        scratch_shapes=[
            pltpu.VMEM((count, 128), F32),
            pltpu.VMEM((1, count), jnp.int32),
            pltpu.VMEM((entries, count), jnp.int32),
            pltpu.SemaphoreType.DMA((5,)),
        ],
        compiler_params=pltpu.CompilerParams(vmem_limit_bytes=LIMIT),
        name="pack",
    )(*map(in_hbm, (jnp.transpose(positions, (1, 0, 2)), charges, right_side, owners.T, neighbours.T)))

    def both_sides(value):
        far = lax.ppermute(value, "slab", outer)
        near = lax.ppermute(value, "slab", inner)
        return near, far

    scale = 8.0 / ((entries + 1) * 128)
    near, far = both_sides(packed)
    own_blocks, total, coupled = own_weights(packed, scale)
    blocks, first, diagonal, row = other_weights(
        index, packed, near, far, total, coupled, drag, scale, entries
    )
    near, far = both_sides(first)
    coupled = own_image(first, own_blocks)
    second, row = image(index, blocks, coupled, diagonal, row, near, far, packed, [first])
    near, far = both_sides(second)
    coupled = own_image(second, own_blocks)
    third, row = image(
        index, blocks, coupled, diagonal, row, near, far, packed, [first, second]
    )
    row = row + lax.ppermute(row, "slab", inner)
    around = [
        lax.ppermute(row, "slab", [(i, (i + step) % slab_count) for i in range(slab_count)])
        for step in range(2, slab_count, 2)
    ]
    outgoing = jax.ShapeDtypeStruct((brick_count, 4 * each + 8, 128), F32)
    params = pltpu.CompilerParams(vmem_limit_bytes=LIMIT)
    basis = pl.pallas_call(
        slots_kernel,
        out_shape=outgoing,
        in_specs=[VMEM] * 5,
        out_specs=VMEM,
        compiler_params=params,
        cost_estimate=pl.CostEstimate(flops=1 << 30, bytes_accessed=1 << 20, transcendentals=0),
        name="slots",
    )(target, packed, first, second, third)
    outgoing = pl.pallas_call(
        join_kernel,
        out_shape=outgoing,
        in_specs=[VMEM] * (2 + len(around)),
        out_specs=VMEM,
        input_output_aliases={1 + len(around): 0},
        compiler_params=params,
        name="join",
    )(row, *around, basis)
    arrived = lax.all_to_all(outgoing, "brick", split_axis=0, concat_axis=0, tiled=True)
    shape = jax.ShapeDtypeStruct((brick_count * each, 128), F32)
    return pl.pallas_call(
        finish_kernel,
        out_shape=(shape, shape),
        in_specs=[VMEM],
        out_specs=(HBM, HBM),
        scratch_shapes=[
            pltpu.VMEM(shape.shape, F32),
            pltpu.VMEM(shape.shape, F32),
            pltpu.SemaphoreType.DMA((2, 4)),
        ],
        compiler_params=pltpu.CompilerParams(vmem_limit_bytes=LIMIT),
        name="finish",
    )(arrived)


def solution(mesh):
    placed = (
        P(BOTH, None, None),
        P(BOTH, None),
        P(BOTH, None),
        P(BOTH, None),
        P(BOTH, None),
        P(BOTH, None),
    )
    step = jax.shard_map(
        local,
        mesh=mesh,
        in_specs=placed,
        out_specs=(P(BOTH, None), P(BOTH, None)),
        check_vma=False,
    )
    return step
```
